128 devices in a mesh: ctx: 32 (over x, y, core), heads: 4 (over z).
Axes of the slice: x: 4, y: 4, z: 4, core: 2. Of those that a mesh axis runs over, the one named last changes fastest.
Arguments:
- queries: bfloat16 [32, 32768, 128], P('heads', 'ctx'), may hold values from -6 to 6
- keys: bfloat16 [32, 32768, 128], P('heads', 'ctx'), may hold values from -6 to 6
- values: bfloat16 [32, 32768, 128], P('heads', 'ctx'), may hold values from -6 to 6
- out_grad: bfloat16 [32, 32768, 128], P('heads', 'ctx'), may hold values from -6 to 6
- level_table: float32 [64, 16], replicated, may hold values from 0.2 to 2
- table_index: int32 [32768], P('ctx'), may hold values from 0 to 63
Outputs:
- attention_out: bfloat16 [32, 32768, 128], P('heads', 'ctx')
- query_grad: bfloat16 [32, 32768, 128], P('heads', 'ctx')
- key_grad: bfloat16 [32, 32768, 128], P('heads', 'ctx')
- value_grad: bfloat16 [32, 32768, 128], P('heads', 'ctx')
- table_grad: float32 [64, 16], replicated
The draws below stay inside these ranges and needn't reach their ends.
All inputs are finite; a program needn't handle non-finite values.
Results may differ from the reference program's by a relative error of at most 0.0058.
Values sent between devices are 32-bit elements; how exact they have to be, the bound alone decides.
A program may use at most 256 MiB of HBM per device.

```python
import math
import jax
import jax.numpy as jnp
from jax import lax

HEADS = 32
DH = 128
TOK_DEV = 1024
TABLE = 64
LEVELS = 16
TOKENS = 32768
N_CTX = 32


def touch_ends(values, key, least, high):
    dims = values.shape
    spot = [jax.random.randint(jax.random.fold_in(key, axis), (), 0, dims[axis]) for axis in range(len(dims))]
    values = values.at[tuple(spot)].set(least)
    longest = dims.index(max(dims))
    spot[longest] = (spot[longest] + 1) % dims[longest]
    return values.at[tuple(spot)].set(high)


def steps_of(rng, extent, cuts, low, high):
    def one(dim, blocks):
        heights = jax.random.uniform(jax.random.fold_in(jax.random.fold_in(rng, 6), dim), (blocks,), jnp.float32, low / len(cuts), high / len(cuts))
        return jnp.repeat(jnp.exp(heights), extent[dim] // blocks).reshape((-1,) + (1,) * (len(extent) - dim - 1))

    level = one(*cuts[0])
    for cut in cuts[1:]:
        level = level * one(*cut)
    return level


def noise(rng, shape, deviation, reach, shards=(), kind=jnp.bfloat16):
    factor_of = steps_of(rng, shape, shards, -0.22, 0.18) if shards else 1.0
    drawn = jax.random.normal(rng, shape, jnp.float32) * deviation * factor_of
    return jnp.minimum(jnp.maximum(drawn, -reach), reach).astype(kind)


def setup_inputs(seed: int = 0) -> dict:
    streams_of = jax.random.split(jax.random.key(seed), 7)
    queries = noise(streams_of[0], (HEADS, TOKENS, DH), 1.0, 6.0, ((0, 4), (1, 32)))
    keys = noise(streams_of[1], (HEADS, TOKENS, DH), 1.0, 6.0, ((0, 4), (1, 32)))
    values = noise(streams_of[2], (HEADS, TOKENS, DH), 1.0, 6.0, ((0, 4), (1, 32)))
    out_grad = noise(streams_of[3], (HEADS, TOKENS, DH), 1.0, 6.0, ((0, 4), (1, 32)))
    level_table = jnp.clip(jnp.exp(jax.random.uniform(streams_of[4], (TABLE, LEVELS), jnp.float32, math.log(0.2), math.log(2.0))), 0.2, 2.0)
    table_index = touch_ends(jax.random.randint(streams_of[5], (TOKENS,), 0, TABLE), jax.random.fold_in(streams_of[5], 1), 0, TABLE - 1).astype(jnp.int32)
    return dict(queries=queries, keys=keys, values=values, out_grad=out_grad, level_table=level_table, table_index=table_index)


HIGHEST = lax.Precision.HIGHEST

def level_grid(length):
    row_ids = lax.broadcasted_iota(jnp.int32, (length, length), 0)
    col_ids = lax.broadcasted_iota(jnp.int32, (length, length), 1)
    crossed = jnp.bitwise_xor(row_ids, col_ids)
    levels = jnp.zeros((length, length), jnp.int32)
    for bit_pos in range(length.bit_length()):
        levels = levels + (crossed >= 1 << bit_pos).astype(jnp.int32)
    return (levels, col_ids <= row_ids)

def lookup(level_table, table_index):
    matches = table_index[:, None] == jnp.arange(level_table.shape[0], dtype=jnp.int32)[None, :]
    lam_all = lax.optimization_barrier(jnp.sum(jnp.where(matches[:, :, None], level_table[None], 0.0), 1))
    return (matches, lam_all)

def block_start(queries, keys, values, out_grad, lam_tok, block_id, level_bits, factor):
    first_cross = queries.shape[1].bit_length()
    states = jnp.einsum('htd,hte->hde', keys.astype(jnp.float32), values.astype(jnp.float32))
    pieces = []
    for bit_num in range(level_bits):
        scaled = (lam_tok[:, first_cross + bit_num][None, :, None] * out_grad).astype(jnp.bfloat16)
        upper_half = jnp.right_shift(block_id, bit_num) & 1 == 1
        bucket_grad = factor * jnp.einsum('htd,hte->hde', queries.astype(jnp.float32), scaled.astype(jnp.float32))
        pieces.append(jnp.where(upper_half, bucket_grad, jnp.zeros_like(bucket_grad)))
    return (states, jnp.stack(pieces))

def block_finish(queries, keys, values, out_grad, lam_tok, bucket, state_grad, factor):
    length = queries.shape[1]
    level_bits = bucket.shape[0]
    first_cross = length.bit_length()
    levels, causal = level_grid(length)
    weight = jnp.zeros((length, length), jnp.float32)
    for level_id in range(first_cross):
        weight = weight + jnp.where(levels == level_id, lam_tok[:, level_id:level_id + 1], 0.0)
    weight = jnp.where(causal, weight, 0.0)

    def one_head(summed, per_head):
        head_query, head_keys, head_values, head_grad = per_head
        dot_scores = jnp.dot(head_query, head_keys.T, preferred_element_type=jnp.float32)
        weighted = (factor * weight * dot_scores).astype(jnp.bfloat16)
        out_local = jnp.dot(weighted, head_values, preferred_element_type=jnp.float32)
        grad_weighted = jnp.dot(head_grad, head_values.T, preferred_element_type=jnp.float32)
        grad_scores = (factor * weight * grad_weighted).astype(jnp.bfloat16)
        query_local = jnp.dot(grad_scores, head_keys, preferred_element_type=jnp.float32)
        key_local = jnp.dot(grad_scores.T, head_query, preferred_element_type=jnp.float32)
        value_local = jnp.dot(weighted.T, head_grad, preferred_element_type=jnp.float32)
        return (summed + dot_scores * grad_weighted, (out_local, query_local, key_local, value_local))
    start_sum = jnp.zeros((length, length), jnp.float32)
    weight_grad, (out_local, query_local, key_local, value_local) = lax.scan(one_head, start_sum, (queries, keys, values, out_grad))
    lam_cross = lam_tok[:, first_cross:first_cross + level_bits].T[:, None, :, None]
    cross = jnp.einsum('htd,jhde->jhte', queries.astype(jnp.float32), bucket.astype(jnp.float32))
    attention_out = out_local + factor * lax.optimization_barrier(jnp.sum(lam_cross * cross, 0))
    back_cross = jnp.einsum('hte,jhde->jhtd', out_grad.astype(jnp.float32), bucket.astype(jnp.float32))
    query_grad = query_local + factor * lax.optimization_barrier(jnp.sum(lam_cross * back_cross, 0))
    key_grad = key_local + jnp.einsum('hte,hde->htd', values.astype(jnp.float32), state_grad.astype(jnp.float32))
    value_grad = value_local + jnp.einsum('htd,hde->hte', keys.astype(jnp.float32), state_grad.astype(jnp.float32))
    local_cols = [factor * lax.optimization_barrier(jnp.sum(jnp.where(causal & (levels == level_id), weight_grad, 0.0), 1)) for level_id in range(first_cross)]
    lam_local = jnp.stack(local_cols, 1)
    lam_far = factor * lax.optimization_barrier(jnp.sum(cross * out_grad.astype(jnp.float32)[None], axis=(1, 3)))
    spare = jnp.zeros((length, lam_tok.shape[1] - first_cross - level_bits), jnp.float32)
    lam_grad = jnp.concatenate([lam_local, lam_far.T, spare], 1)
    return (attention_out.astype(jnp.bfloat16), query_grad.astype(jnp.bfloat16), key_grad.astype(jnp.bfloat16), value_grad.astype(jnp.bfloat16), lam_grad)

def bucket_sums(states, level_bits):
    blocks = states.shape[0]
    rest = states.shape[1:]
    pieces = []
    for bit_num in range(level_bits):
        grouped = states.reshape((blocks >> bit_num + 1, 2, 1 << bit_num) + rest)
        lower_half = lax.optimization_barrier(jnp.sum(grouped[:, 0], axis=1, keepdims=True))
        upper_fill = jnp.broadcast_to(lower_half, grouped[:, 1].shape)
        filled = jnp.stack([jnp.zeros_like(upper_fill), upper_fill], 1)
        pieces.append(filled.reshape(states.shape))
    return jnp.stack(pieces, 1)

def grad_sums(grads, level_bits):
    blocks = grads.shape[0]
    rest = grads.shape[2:]
    summed = jnp.zeros((blocks,) + rest, jnp.float32)
    for bit_num in range(level_bits):
        grouped = grads[:, bit_num].reshape((blocks >> bit_num + 1, 2, 1 << bit_num) + rest)
        upper_half = lax.optimization_barrier(jnp.sum(grouped[:, 1], axis=1, keepdims=True))
        lower_fill = jnp.broadcast_to(upper_half, grouped[:, 0].shape)
        filled = jnp.stack([lower_fill, jnp.zeros_like(lower_fill)], 1)
        summed = summed + filled.reshape(summed.shape)
    return summed

def reference(queries, keys, values, out_grad, level_table, table_index):
    head_count, tokens, head_width = queries.shape
    length = TOK_DEV
    blocks = N_CTX
    level_bits = blocks.bit_length() - 1
    factor = 1.0 / math.sqrt(head_width * tokens)
    matches, lam_all = lookup(level_table, table_index)

    def by_block(array):
        return array.reshape(head_count, blocks, length, head_width).transpose(1, 0, 2, 3)
    block_query = by_block(queries)
    block_keys = by_block(keys)
    block_values = by_block(values)
    block_grad = by_block(out_grad)
    block_lam = lam_all.reshape(blocks, length, lam_all.shape[1])
    block_ids = jnp.arange(blocks, dtype=jnp.int32)

    def first_pass(packed):
        return block_start(packed[0], packed[1], packed[2], packed[3], packed[4], packed[5], level_bits, factor)
    states, grads = lax.map(first_pass, (block_query, block_keys, block_values, block_grad, block_lam, block_ids))
    bucket = bucket_sums(states, level_bits).astype(jnp.bfloat16)
    state_grad = grad_sums(grads, level_bits).astype(jnp.bfloat16)

    def second_pass(packed):
        return block_finish(packed[0], packed[1], packed[2], packed[3], packed[4], packed[5], packed[6], factor)
    results = lax.map(second_pass, (block_query, block_keys, block_values, block_grad, block_lam, bucket, state_grad))

    def joined(array):
        return array.transpose(1, 0, 2, 3).reshape(head_count, tokens, head_width)
    lam_grad = results[4].reshape(tokens, lam_all.shape[1])
    table_grad = lax.optimization_barrier(jnp.sum(jnp.where(matches[:, :, None], lam_grad[:, None, :], 0.0), 0)) / math.sqrt(tokens)
    return (joined(results[0]), joined(results[1]), joined(results[2]), joined(results[3]), table_grad)
```

```python
import functools
import math

import jax
import jax.numpy as jnp
from jax import lax
from jax.experimental import pallas as pl
from jax.experimental.pallas import tpu as pltpu
from jax.sharding import PartitionSpec as P

SUB = 256
F32 = jnp.float32
BF16 = jnp.bfloat16
NN = (((1,), (0,)), ((), ()))
NT = (((1,), (1,)), ((), ()))
TN = (((0,), (0,)), ((), ()))


def mm(a, b, dims):
    return lax.dot_general(a, b, dims, preferred_element_type=F32)


def split3(value):
    first = value.astype(BF16)
    rest = value - first.astype(F32)
    second = rest.astype(BF16)
    third = (rest - second.astype(F32)).astype(BF16)
    return first, second, third


def one_hot(index_row, rows):
    length = index_row.shape[1]
    row_ids = lax.broadcasted_iota(jnp.int32, (rows, length), 0)
    return jnp.where(row_ids == index_row, 1.0, 0.0).astype(BF16)


def fill_lambda(index_ref, table_ref, wide_ref, diag_ref, factor):
    hot = one_hot(index_ref[...], table_ref.shape[0])
    parts = split3(table_ref[...] * factor)
    lam = sum(mm(hot, part, TN) for part in parts)
    length = lam.shape[0]
    for level in range(wide_ref.shape[0]):
        column = lam[:, 9 + level : 10 + level]
        wide_ref[level] = jnp.broadcast_to(column, (length, 128))
    rows = lax.broadcasted_iota(jnp.int32, (SUB, SUB), 0)
    cols = lax.broadcasted_iota(jnp.int32, (SUB, SUB), 1)
    crossed = jnp.bitwise_xor(rows, cols)
    for tile in range(length // SUB):
        part = lam[tile * SUB : (tile + 1) * SUB]
        weight = jnp.broadcast_to(part[:, 0:1], (SUB, SUB))
        for level in range(1, 9):
            weight = jnp.where(crossed >= 1 << (level - 1), part[:, level : level + 1], weight)
        diag_ref[tile] = jnp.where(cols <= rows, weight, 0.0)


def pre_kernel(q_ref, k_ref, v_ref, g_ref, index_ref, table_ref, state_ref, grad_ref, wide, diag, *, factor):
    head = pl.program_id(0)

    @pl.when(head == 0)
    def _():
        fill_lambda(index_ref, table_ref, wide, diag, factor)

    state_ref[0] = mm(k_ref[0], v_ref[0], TN)
    grad = g_ref[0].astype(F32)
    block_id = lax.axis_index("ctx")
    scaled = jnp.concatenate([(wide[2 + j] * grad).astype(BF16) for j in range(5)], axis=1)
    total = mm(q_ref[0], scaled, TN)
    for j in range(5):
        keep = (block_id >> j) & 1 == 1
        grad_ref[j, 0] = jnp.where(keep, total[:, j * 128 : (j + 1) * 128], 0.0)


def main_kernel(
    q_ref, k_ref, v_ref, g_ref, index_ref, table_ref, bucket_ref, sgrad_ref,
    out_ref, qg_ref, kg_ref, vg_ref, part_ref,
    wide, diag, wsum, lsum, *, factor,
):
    head = pl.program_id(0)

    @pl.when(head == 0)
    def _():
        fill_lambda(index_ref, table_ref, wide, diag, factor)
        wsum[...] = jnp.zeros_like(wsum)
        lsum[...] = jnp.zeros_like(lsum)

    tiles = q_ref.shape[1] // SUB
    states = [mm(k_ref[0, pl.ds(c * SUB, SUB)], v_ref[0, pl.ds(c * SUB, SUB)], TN) for c in range(3)]
    near = {1: states[0].astype(BF16), 3: states[2].astype(BF16)}
    pair = (states[0] + states[1]).astype(BF16)
    far_bucket = bucket_ref[0].astype(BF16)
    far_grad = sgrad_ref[0]
    near_grad = {}
    pair_grad = None
    for c in range(tiles):
        rows = pl.ds(c * SUB, SUB)
        q, grad = q_ref[0, rows], g_ref[0, rows]
        wide_grad = grad.astype(F32)
        use = ([0] if c % 2 else []) + ([1] if c >= 2 else [])
        for level in use:
            scaled = (wide[level, rows] * wide_grad).astype(BF16)
            value = mm(q, scaled, TN)
            if level == 0:
                near_grad[c - 1] = value
            else:
                pair_grad = value if pair_grad is None else pair_grad + value
    for c in range(tiles):
        rows = pl.ds(c * SUB, SUB)
        q, k, v, grad = q_ref[0, rows], k_ref[0, rows], v_ref[0, rows], g_ref[0, rows]
        wide_grad = grad.astype(F32)
        score = mm(q, k, NT)
        back = mm(grad, v, NT)
        wsum[c] += score * back
        weight = diag[c]
        weighted = (weight * score).astype(BF16)
        dscore = (weight * back).astype(BF16)
        out = mm(weighted, v, NN)
        qg = mm(dscore, k, NN)
        kg = mm(dscore, q, TN)
        vg = mm(weighted, grad, TN)
        use = ([0] if c % 2 else []) + ([1] if c >= 2 else []) + [2, 3, 4, 5, 6]
        buckets = ([near[c]] if c % 2 else []) + ([pair] if c >= 2 else []) + [far_bucket]
        joined = jnp.concatenate(buckets, axis=1)
        cross = mm(q, joined, NN)
        scaled = []
        for n, level in enumerate(use):
            piece = cross[:, n * 128 : (n + 1) * 128]
            lam = wide[level, rows]
            out += lam * piece
            lsum[level, rows] += piece * wide_grad
            scaled.append((lam * wide_grad).astype(BF16))
        qg += mm(jnp.concatenate(scaled, axis=1), joined, NT)
        dstate = far_grad
        if c in near_grad:
            dstate = dstate + near_grad[c]
        if c < 2:
            dstate = dstate + pair_grad
        dstate = dstate.astype(BF16)
        kg += mm(v, dstate, NT)
        vg += mm(k, dstate, NN)
        out_ref[0, rows] = out.astype(BF16)
        qg_ref[0, rows] = qg.astype(BF16)
        kg_ref[0, rows] = kg.astype(BF16)
        vg_ref[0, rows] = vg.astype(BF16)

    @pl.when(head == pl.num_programs(0) - 1)
    def _():
        hot = one_hot(index_ref[...], table_ref.shape[0])
        lane = lax.broadcasted_iota(jnp.int32, part_ref.shape, 1)
        rows = lax.broadcasted_iota(jnp.int32, (SUB, SUB), 0)
        cols = lax.broadcasted_iota(jnp.int32, (SUB, SUB), 1)
        crossed = jnp.bitwise_xor(rows, cols)
        table = jnp.zeros(part_ref.shape, F32)
        for level in range(16):
            if level < 9:
                total = jnp.zeros((table_ref.shape[0], 128), F32)
                low = (1 << (level - 1)) if level else 0
                mask = (crossed >= low) & (crossed < (1 << level)) & (cols <= rows)
                for c in range(tiles):
                    value = jnp.where(mask, wsum[c], 0.0)
                    value = value[:, :128] + value[:, 128:]
                    high, rest, _ = split3(value)
                    part = hot[:, c * SUB : (c + 1) * SUB]
                    total += mm(part, high, NN) + mm(part, rest, NN)
            else:
                high, rest, _ = split3(lsum[level - 9])
                total = mm(hot, high, NN) + mm(hot, rest, NN)
            column = jnp.sum(total, axis=1, keepdims=True)
            table = jnp.where(lane == level, column, table)
        part_ref[...] = table * factor


def body(queries, keys, values, out_grad, level_table, table_index):
    heads, length, width = queries.shape
    devices = lax.axis_size("ctx")
    factor = 1.0 / math.sqrt(width * length * devices)
    index_row = table_index.reshape(1, length)
    block = pl.BlockSpec((1, length, width), lambda h: (h, 0, 0))
    whole = lambda shape: pl.BlockSpec(shape, lambda h: (0,) * len(shape))
    scratch = [
        pltpu.VMEM((7, length, 128), F32),
        pltpu.VMEM((length // SUB, SUB, SUB), F32),
    ]
    params = pltpu.CompilerParams(
        dimension_semantics=("arbitrary",), vmem_limit_bytes=60 << 20
    )
    states, grads = pl.pallas_call(
        functools.partial(pre_kernel, factor=factor),
        grid=(heads,),
        out_shape=(
            jax.ShapeDtypeStruct((heads, width, width), F32),
            jax.ShapeDtypeStruct((5, heads, width, width), F32),
        ),
        in_specs=[block] * 4 + [whole(index_row.shape), whole(level_table.shape)],
        out_specs=(
            pl.BlockSpec((1, width, width), lambda h: (h, 0, 0)),
            pl.BlockSpec((5, 1, width, width), lambda h: (0, h, 0, 0)),
        ),
        scratch_shapes=scratch,
        compiler_params=params,
    )(queries, keys, values, out_grad, index_row, level_table)
    block_id = lax.axis_index("ctx")
    steps = (1, 2, 6, 8, 24)
    swap = lambda value, step: lax.ppermute(value, "ctx", [(b, b ^ step) for b in range(devices)])
    tree = states
    pieces = []
    dtree = jnp.zeros_like(states)
    received = [None] * 5
    for j, step in enumerate(steps):
        other = swap(tree, step)
        pieces.append(jnp.where((block_id >> j) & 1 == 1, other, 0.0))
        tree = tree + other
        back = 4 - j
        dtree = dtree + swap(dtree + grads[back], steps[back])
    bucket = jnp.concatenate(pieces, axis=-1)
    outs = pl.pallas_call(
        functools.partial(main_kernel, factor=factor),
        grid=(heads,),
        out_shape=tuple(jax.ShapeDtypeStruct(queries.shape, BF16) for _ in range(4))
        + (jax.ShapeDtypeStruct(level_table.shape, F32),),
        in_specs=[block] * 4
        + [
            whole(index_row.shape),
            whole(level_table.shape),
            pl.BlockSpec((1, width, 5 * width), lambda h: (h, 0, 0)),
            pl.BlockSpec((1, width, width), lambda h: (h, 0, 0)),
        ],
        out_specs=(block,) * 4 + (whole(level_table.shape),),
        scratch_shapes=scratch
        + [
            pltpu.VMEM((length // SUB, SUB, SUB), F32),
            pltpu.VMEM((7, length, 128), F32),
        ],
        compiler_params=params,
    )(queries, keys, values, out_grad, index_row, level_table, bucket, dtree)
    table_total = lax.psum(outs[4], ("ctx", "heads"))
    table_grad = table_total / math.sqrt(length * devices)
    return outs[:4] + (table_grad,)


def solution(mesh):
    placed = (P("heads", "ctx", None),) * 4
    return jax.shard_map(
        body,
        mesh=mesh,
        in_specs=placed + (P(), P("ctx")),
        out_specs=placed + (P(),),
        check_vma=False,
    )
```

```python
import functools
import math

import jax
import jax.numpy as jnp
from jax import lax
from jax.experimental import pallas as pl
from jax.experimental.pallas import tpu as pltpu
from jax.sharding import PartitionSpec as P

SUB = 256
PIECES = 2
MESH = pl.DeviceIdType.MESH
F32 = jnp.float32
BF16 = jnp.bfloat16
NN = (((1,), (0,)), ((), ()))
NT = (((1,), (1,)), ((), ()))
TN = (((0,), (0,)), ((), ()))
TT = (((0,), (1,)), ((), ()))


def mm(a, b, dims):
    return lax.dot_general(a, b, dims, preferred_element_type=F32)


def split3(value):
    first = value.astype(BF16)
    rest = value - first.astype(F32)
    second = rest.astype(BF16)
    third = (rest - second.astype(F32)).astype(BF16)
    return first, second, third


def one_hot(index_row, rows):
    length = index_row.shape[1]
    row_ids = lax.broadcasted_iota(jnp.int32, (rows, length), 0)
    return jnp.where(row_ids == index_row, 1.0, 0.0).astype(BF16)


def fill_lambda(hot, table_ref, wide_ref, diag_ref, factor):
    parts = split3(table_ref[...] * factor)
    lam = sum(mm(hot, part, TT) for part in parts)
    length = lam.shape[0]
    for level in range(wide_ref.shape[0]):
        column = lam[:, 9 + level : 10 + level]
        wide_ref[level] = jnp.broadcast_to(column, (length, 128))
    rows = lax.broadcasted_iota(jnp.int32, (SUB, SUB), 0)
    cols = lax.broadcasted_iota(jnp.int32, (SUB, SUB), 1)
    crossed = jnp.bitwise_xor(rows, cols)
    for tile in range(length // SUB):
        part = lam[tile * SUB : (tile + 1) * SUB]
        weight = jnp.broadcast_to(part[:, 0:1], (SUB, SUB))
        for level in range(1, 9):
            weight = jnp.where(crossed >= 1 << (level - 1), part[:, level : level + 1], weight)
        diag_ref[tile] = jnp.where(cols <= rows, weight, 0.0)


def row_sums(hot, value):
    high, rest, _ = split3(value)
    total = mm(hot, high, NN) + mm(hot, rest, NN)
    return jnp.sum(total, axis=1, keepdims=True)


def kernel(
    q_hbm, k_hbm, v_hbm, g_hbm, index_ref, table_ref,
    out_hbm, qg_hbm, kg_hbm, vg_hbm, total_ref,
    qb, kb, vb, gb, lout, lq, lk, lv, wide, diag, wsum, lsum, near, part, cat,
    states, sother, grads, gother, g0other, tree, recv, dsend, drecv, dtree, psum,
    in_sem, out_sem, s_send, s_recv, g_send, g_recv, f_send, f_recv, r_send, r_recv,
    b_send, b_recv, d_send, d_recv, p_send, p_recv,
    *, factor, scale,
):
    heads, length, _ = qb.shape
    tiles = length // SUB
    half = heads // 2
    unit = half // PIECES
    me = lax.axis_index("ctx")
    z = lax.axis_index("heads")
    core = me % 2
    y = (me // 2) % 4
    x = me // 8
    mine = core * half
    theirs = (1 - core) * half
    sibling = me + 1 - 2 * core
    at = lambda px, py: (px * 4 + py) * 2 + core
    hops = (at(x, y + 1 - 2 * (y % 2)), at(x, 3 - y), at(x + 1 - 2 * (x % 2), y), at(3 - x, y))
    bits = (core == 1, y % 2 == 1, y // 2 == 1, x % 2 == 1, x // 2 == 1)

    def pick(level):
        return jnp.where(level == 0, hops[0], jnp.where(level == 1, hops[1], jnp.where(level == 2, hops[2], hops[3])))

    def remote(src, dst, send, got, device):
        return pltpu.make_async_remote_copy(
            src_ref=src, dst_ref=dst, send_sem=send, recv_sem=got, device_id=device, device_id_type=MESH
        )

    loads = ((kb, k_hbm), (vb, v_hbm), (qb, q_hbm), (gb, g_hbm))

    def load(n, h):
        return pltpu.make_async_copy(loads[n][1].at[h], loads[n][0].at[h], in_sem.at[n, h])

    def start_loads(first):
        def step(i, carry):
            h = lax.rem(theirs + i, heads)
            load(first, h).start()
            load(first + 1, h).start()
            return carry

        lax.fori_loop(0, heads, step, 0)

    start_loads(0)
    start_loads(2)

    barrier = pltpu.get_barrier_semaphore()
    pl.semaphore_signal(barrier, inc=1, device_id={"ctx": sibling}, device_id_type=MESH)
    for d in range(1, 4):
        pl.semaphore_signal(barrier, inc=1, device_id={"ctx": at(x, (y + d) % 4)}, device_id_type=MESH)
        pl.semaphore_signal(barrier, inc=1, device_id={"ctx": at((x + d) % 4, y)}, device_id_type=MESH)
        pl.semaphore_signal(barrier, inc=1, device_id={"heads": (z + d) % 4}, device_id_type=MESH)

    hot = one_hot(index_ref[...], table_ref.shape[1])
    fill_lambda(hot, table_ref, wide, diag, factor)

    def state_step(i, carry):
        h = lax.rem(theirs + i, heads)
        load(0, h).wait()
        load(1, h).wait()
        s = [mm(kb[h, pl.ds(c * SUB, SUB)], vb[h, pl.ds(c * SUB, SUB)], TN) for c in range(tiles)]
        pair = s[0] + s[1]
        near[h, 0] = s[0].astype(BF16)
        near[h, 1] = s[2].astype(BF16)
        near[h, 2] = pair.astype(BF16)
        states[h] = pair + (s[2] + s[3])
        return carry

    lax.fori_loop(0, heads, state_step, 0)
    pl.semaphore_wait(barrier, 10)

    def state_copy(n, low):
        block = pl.ds(low, half)
        return remote(states.at[block], sother.at[block], s_send.at[n], s_recv.at[n], {"ctx": sibling})

    state_copy(0, theirs).start()
    state_copy(1, mine).start()
    wsum[...] = jnp.zeros_like(wsum)
    lsum[...] = jnp.zeros_like(lsum)

    def grad_step(i, carry):
        h = lax.rem(theirs + i, heads)
        load(2, h).wait()
        load(3, h).wait()
        total = None
        for c in range(tiles):
            rows = pl.ds(c * SUB, SUB)
            wide_grad = gb[h, rows].astype(F32)
            scaled = jnp.concatenate([(wide[2 + j, rows] * wide_grad).astype(BF16) for j in range(5)], axis=1)
            value = mm(qb[h, rows], scaled, TN)
            total = value if total is None else total + value
        for j in range(5):
            grads[j, h] = jnp.where(bits[j], total[:, j * 128 : (j + 1) * 128], 0.0)
        return carry

    def tree_copy(level, u):
        src = tree.at[level, pl.ds(u * unit, unit)]
        dst = recv.at[level, pl.ds(mine + u * unit, unit)]
        return remote(src, dst, f_send.at[level, u], f_recv.at[level, u], {"ctx": pick(level)})

    def relay(level, u, low):
        block = recv.at[level, pl.ds(low + u * unit, unit)]
        return remote(block, block, r_send.at[level, u], r_recv.at[level, u], {"ctx": sibling})

    def dtree_copy(level, u):
        block = pl.ds(u * unit, unit)
        return remote(dsend.at[level, block], drecv.at[level, block], b_send.at[level, u], b_recv.at[level, u], {"ctx": pick(level)})

    def dtree_relay(u, low):
        block = dtree.at[pl.ds(low + u * unit, unit)]
        return remote(block, block, d_send.at[u], d_recv.at[u], {"ctx": sibling})

    def grad_copy(j):
        return remote(grads.at[j, pl.ds(theirs, half)], gother.at[j - 1], g_send.at[j], g_recv.at[j], {"ctx": sibling})

    def grad0_copy():
        return remote(grads.at[0], g0other, g_send.at[0], g_recv.at[0], {"ctx": sibling})

    lax.fori_loop(0, half, grad_step, 0)
    state_copy(0, mine).wait_recv()
    tree[0] = states[pl.ds(mine, half)] + sother[pl.ds(mine, half)]
    for j in (4, 3, 2, 1):
        grad_copy(j).start()
    for u in range(PIECES):
        tree_copy(0, u).start()
    lax.fori_loop(half, heads, grad_step, 0)
    grad0_copy().start()
    grad_copy(4).wait_recv()
    dsend[3] = grads[4, pl.ds(mine, half)] + gother[3]
    for u in range(PIECES):
        dtree_copy(3, u).start()

    def comm_step(step):
        level = step // PIECES
        u = step % PIECES
        back = 3 - level
        block = pl.ds(u * unit, unit)
        own = pl.ds(mine + u * unit, unit)

        @pl.when((u == 0) & (level < 3))
        def _():
            grad_copy(back).wait_recv()

        tree_copy(level, u).wait_recv()
        relay(level, u, mine).start()
        dtree_copy(back, u).wait_recv()

        @pl.when(level < 3)
        def _():
            tree[level + 1, block] = tree[level, block] + recv[level, own]

        @pl.when(level == 0)
        def _():
            dtree[own] = drecv[back, block]

        @pl.when(level > 0)
        def _():
            dtree[own] = dtree[own] + drecv[back, block]

        @pl.when(level < 3)
        def _():
            dsend[back - 1, block] = dtree[own] + (grads[back, own] + gother[back - 1, block])
            tree_copy(level + 1, u).start()
            dtree_copy(back - 1, u).start()

        @pl.when(level == 3)
        def _():
            dtree_relay(u, mine).start()

    def local_head(h):
        def tile(c):
            rows = pl.ds(c * SUB, SUB)
            return rows, qb[h, rows], kb[h, rows], vb[h, rows], gb[h, rows]

        near_grad = {}
        pair_grad = None
        for c in range(tiles - 1, -1, -1):
            rows, q, k, v, grad = tile(c)
            score = mm(q, k, NT)
            back = mm(grad, v, NT)
            wsum[c] += score * back
            weight = diag[c]
            weighted = (weight * score).astype(BF16)
            dscore = (weight * back).astype(BF16)
            out = mm(weighted, v, NN)
            qg = mm(dscore, k, NN)
            kg = mm(dscore, q, TN)
            vg = mm(weighted, grad, TN)
            use = ([0] if c % 2 else []) + ([1] if c >= 2 else [])
            if use:
                buckets = ([near[h, c // 2]] if c % 2 else []) + ([near[h, 2]] if c >= 2 else [])
                joined = jnp.concatenate(buckets, axis=1)
                cross = mm(q, joined, NN)
                wide_grad = grad.astype(F32)
                scaled = []
                for n, level in enumerate(use):
                    piece = cross[:, n * 128 : (n + 1) * 128]
                    lam = wide[level, rows]
                    out += lam * piece
                    lsum[level, rows] += piece * wide_grad
                    scaled.append((lam * wide_grad).astype(BF16))
                scaled = jnp.concatenate(scaled, axis=1)
                qg += mm(scaled, joined, NT)
                value = mm(q, scaled, TN)
                for n, level in enumerate(use):
                    piece = value[:, n * 128 : (n + 1) * 128]
                    if level == 0:
                        near_grad[c - 1] = piece
                    else:
                        pair_grad = piece if pair_grad is None else pair_grad + piece
            dstate = near_grad.get(c)
            if c < 2:
                dstate = pair_grad if dstate is None else dstate + pair_grad
            if dstate is not None:
                dlocal[c] = dstate
            lout[h, rows] = out
            lq[h, rows] = qg
            lk[h, rows] = kg
            lv[h, rows] = vg
        return dlocal

    dlocal = {}

    def local_step(h, carry):
        @pl.when(h > 0)
        def _():
            comm_step(h - 1)

        local_head(h)
        for c in range(3):
            part[h, c] = dlocal[c]
        return carry

    lax.fori_loop(0, heads, local_step, 0)

    lane = lax.broadcasted_iota(jnp.int32, (table_ref.shape[1], 128), 1)
    hot = one_hot(index_ref[...], table_ref.shape[1])
    rows_id = lax.broadcasted_iota(jnp.int32, (SUB, SUB), 0)
    cols_id = lax.broadcasted_iota(jnp.int32, (SUB, SUB), 1)
    crossed = jnp.bitwise_xor(rows_id, cols_id)
    table = jnp.zeros(lane.shape, F32)
    for level in range(11):
        if level < 9:
            low = (1 << (level - 1)) if level else 0
            mask = (crossed >= low) & (crossed < (1 << level)) & (cols_id <= rows_id)
            values = []
            for c in range(tiles):
                value = jnp.where(mask, wsum[c], 0.0)
                values.append(value[:, :128] + value[:, 128:])
            value = jnp.concatenate(values, axis=0)
        else:
            value = lsum[level - 9]
        table = jnp.where(lane == level, row_sums(hot, value), table)

    for step in range(heads - 1, 4 * PIECES):
        comm_step(step)

    state_copy(1, theirs).wait_recv()
    for level in range(4):
        for u in range(PIECES):
            relay(level, u, theirs).wait_recv()

    stores = ((qb, out_hbm), (gb, qg_hbm), (vb, kg_hbm), (kb, vg_hbm))

    def store(n, h):
        return pltpu.make_async_copy(stores[n][0].at[h], stores[n][1].at[h], out_sem.at[n, h])

    def cross_step(h, carry):
        cat[h, :, 0:128] = jnp.where(bits[0], sother[h], 0.0).astype(BF16)
        for j in range(1, 5):
            cat[h, :, j * 128 : (j + 1) * 128] = jnp.where(bits[j], recv[j - 1, h], 0.0).astype(BF16)
        joined = cat[h]
        for c in range(tiles):
            rows = pl.ds(c * SUB, SUB)
            cross = mm(qb[h, rows], joined, NN)
            wide_grad = gb[h, rows].astype(F32)
            out = lout[h, rows]
            for j in range(5):
                piece = cross[:, j * 128 : (j + 1) * 128]
                out += wide[2 + j, rows] * piece
                lsum[2 + j, rows] += piece * wide_grad
            qb[h, rows] = out.astype(BF16)
        store(0, h).start()
        return carry

    lax.fori_loop(0, heads, cross_step, 0)
    for level in range(11, 16):
        table = jnp.where(lane == level, row_sums(hot, lsum[level - 9]), table)

    spots = (z, y, x)
    psum[0, z, :, 0:64] = (table * scale).T[0:16]

    def table_copy(phase, d):
        spot = spots[phase]
        other = (spot + d) % 4
        device = (
            {"heads": other},
            {"ctx": at(x, other)},
            {"ctx": at(other, y)},
        )[phase]
        return remote(
            psum.at[phase, spot], psum.at[phase, spot], p_send.at[phase, d - 1], p_recv.at[phase, d - 1], device
        )

    def table_wait(phase, d):
        other = (spots[phase] + 4 - d) % 4
        slot = psum.at[phase, other]
        return remote(slot, slot, p_send.at[phase, d - 1], p_recv.at[phase, d - 1], {"ctx": sibling})

    def core_copy():
        return remote(psum.at[3, core], psum.at[3, core], p_send.at[3, 0], p_recv.at[3, 0], {"ctx": sibling})

    def core_wait():
        slot = psum.at[3, 1 - core]
        return remote(slot, slot, p_send.at[3, 0], p_recv.at[3, 0], {"ctx": sibling})

    for d in range(1, 4):
        table_copy(0, d).start()

    def table_phase(phase):
        for d in range(1, 4):
            table_wait(phase, d).wait_recv()
        value = (psum[phase, 0] + psum[phase, 1]) + (psum[phase, 2] + psum[phase, 3])
        if phase < 2:
            psum[phase + 1, spots[phase + 1]] = value
            for d in range(1, 4):
                table_copy(phase + 1, d).start()
        else:
            psum[3, core] = value
            core_copy().start()

    for u in range(PIECES):
        dtree_relay(u, theirs).wait_recv()
    grad0_copy().wait_recv()

    def grad_head(h):
        joined = cat[h]
        far = dtree[h] + jnp.where(bits[0], 0.0, g0other[h])
        for c in range(tiles):
            rows = pl.ds(c * SUB, SUB)
            wide_grad = gb[h, rows].astype(F32)
            scaled = jnp.concatenate([(wide[2 + j, rows] * wide_grad).astype(BF16) for j in range(5)], axis=1)
            qg = lq[h, rows] + mm(scaled, joined, NT)
            dstate = (far + part[h, c] if c < 3 else far).astype(BF16)
            kg = lk[h, rows] + mm(vb[h, rows], dstate, NT)
            vg = lv[h, rows] + mm(kb[h, rows], dstate, NN)
            gb[h, rows] = qg.astype(BF16)
            vb[h, rows] = kg.astype(BF16)
            kb[h, rows] = vg.astype(BF16)
        for n in range(1, 4):
            store(n, h).start()

    def grad_loop(low, high):
        def step(h, carry):
            grad_head(h)
            return carry

        lax.fori_loop(low, high, step, 0)

    grad_loop(0, 3)
    table_phase(0)
    grad_loop(3, 6)
    table_phase(1)
    grad_loop(6, heads)
    table_phase(2)
    core_wait().wait_recv()
    total_ref[...] = (psum[3, 0] + psum[3, 1])[:, 0:64]

    def drain(h, carry):
        for n in range(4):
            store(n, h).wait()
        return carry

    lax.fori_loop(0, heads, drain, 0)
    state_copy(0, theirs).wait_send()
    state_copy(1, mine).wait_send()
    grad0_copy().wait_send()
    for j in range(1, 5):
        grad_copy(j).wait_send()
    for u in range(PIECES):
        for level in range(4):
            tree_copy(level, u).wait_send()
            relay(level, u, mine).wait_send()
            dtree_copy(level, u).wait_send()
        dtree_relay(u, mine).wait_send()
    for phase in range(3):
        for d in range(1, 4):
            table_copy(phase, d).wait_send()
    core_copy().wait_send()


def body(queries, keys, values, out_grad, level_table, table_index):
    heads, length, width = queries.shape
    devices = lax.axis_size("ctx")
    factor = 1.0 / math.sqrt(width * length * devices)
    tiles = length // SUB
    half = heads // 2
    dma = lambda *shape: pltpu.SemaphoreType.DMA(shape)
    square = (width, width)
    outs = pl.pallas_call(
        functools.partial(kernel, factor=factor, scale=factor / math.sqrt(length * devices)),
        out_shape=tuple(jax.ShapeDtypeStruct(queries.shape, BF16) for _ in range(4))
        + (jax.ShapeDtypeStruct(level_table.shape[::-1], F32),),
        in_specs=[pl.BlockSpec(memory_space=pltpu.HBM)] * 4 + [pl.BlockSpec(memory_space=pltpu.VMEM)] * 2,
        out_specs=(pl.BlockSpec(memory_space=pltpu.HBM),) * 4 + (pl.BlockSpec(memory_space=pltpu.VMEM),),
        scratch_shapes=[pltpu.VMEM(queries.shape, BF16)] * 4
        + [pltpu.VMEM(queries.shape, F32)] * 4
        + [
            pltpu.VMEM((7, length, 128), F32),
            pltpu.VMEM((tiles, SUB, SUB), F32),
            pltpu.VMEM((tiles, SUB, SUB), F32),
            pltpu.VMEM((7, length, 128), F32),
            pltpu.VMEM((heads, 3) + square, BF16),
            pltpu.VMEM((heads, 3) + square, F32),
            pltpu.VMEM((heads, width, 5 * width), BF16),
            pltpu.VMEM((heads,) + square, F32),
            pltpu.VMEM((heads,) + square, F32),
            pltpu.VMEM((5, heads) + square, F32),
            pltpu.VMEM((4, half) + square, F32),
            pltpu.VMEM((heads,) + square, F32),
            pltpu.VMEM((4, half) + square, F32),
            pltpu.VMEM((4, heads) + square, F32),
            pltpu.VMEM((4, half) + square, F32),
            pltpu.VMEM((4, half) + square, F32),
            pltpu.VMEM((heads,) + square, F32),
            pltpu.VMEM((4, 4, 16, 128), F32),
            dma(4, heads), dma(4, heads), dma(2), dma(2), dma(5), dma(5),
            dma(4, PIECES), dma(4, PIECES), dma(4, PIECES), dma(4, PIECES),
            dma(4, PIECES), dma(4, PIECES), dma(PIECES), dma(PIECES), dma(4, 3), dma(4, 3),
        ],
        compiler_params=pltpu.CompilerParams(
            collective_id=0, has_side_effects=True, vmem_limit_bytes=67043328
        ),
    )(queries, keys, values, out_grad, table_index.reshape(1, length), level_table.T)
    return outs[:4] + (outs[4].T,)


def solution(mesh):
    placed = (P("heads", "ctx", None),) * 4
    return jax.shard_map(
        body,
        mesh=mesh,
        in_specs=placed + (P(), P("ctx")),
        out_specs=placed + (P(),),
        check_vma=False,
    )
```

```python
import functools
import math

import jax
import jax.numpy as jnp
from jax import lax
from jax.experimental import pallas as pl
from jax.experimental.pallas import tpu as pltpu
from jax.sharding import PartitionSpec as P

SUB = 256
PARTNERS = 13
TREE_LAG = 1
MESH = pl.DeviceIdType.MESH
F32 = jnp.float32
BF16 = jnp.bfloat16
NN = (((1,), (0,)), ((), ()))
NT = (((1,), (1,)), ((), ()))
TN = (((0,), (0,)), ((), ()))
TT = (((0,), (1,)), ((), ()))


def mm(a, b, dims):
    return lax.dot_general(a, b, dims, preferred_element_type=F32)


def split3(value):
    first = value.astype(BF16)
    rest = value - first.astype(F32)
    second = rest.astype(BF16)
    third = (rest - second.astype(F32)).astype(BF16)
    return first, second, third


def one_hot(index_row, rows):
    length = index_row.shape[1]
    row_ids = lax.broadcasted_iota(jnp.int32, (rows, length), 0)
    return jnp.where(row_ids == index_row, 1.0, 0.0).astype(BF16)


def fill_lambda(hot, table_ref, wide_ref, diag_ref, factor):
    parts = split3(table_ref[...] * factor)
    lam = sum(mm(hot, part, TT) for part in parts)
    length = lam.shape[0]
    for level in range(wide_ref.shape[0]):
        column = lam[:, 9 + level : 10 + level]
        wide_ref[level] = jnp.broadcast_to(column, (length, 128))
    rows = lax.broadcasted_iota(jnp.int32, (SUB, SUB), 0)
    cols = lax.broadcasted_iota(jnp.int32, (SUB, SUB), 1)
    crossed = jnp.bitwise_xor(rows, cols)
    for tile in range(length // SUB):
        part = lam[tile * SUB : (tile + 1) * SUB]
        weight = jnp.broadcast_to(part[:, 0:1], (SUB, SUB))
        for level in range(1, 9):
            weight = jnp.where(crossed >= 1 << (level - 1), part[:, level : level + 1], weight)
        diag_ref[tile] = jnp.where(cols <= rows, weight, 0.0)


def row_sums(hot, value):
    high, rest, _ = split3(value)
    total = mm(hot, high, NN) + mm(hot, rest, NN)
    return jnp.sum(total, axis=1, keepdims=True)


def kernel(
    q_hbm, k_hbm, v_hbm, g_hbm, index_ref, table_ref,
    out_ref, qg_ref, kg_ref, vg_ref, total_ref,
    qb, kb, vb, gb, lout, lq, lk, lv, wide, diag, wsum, lsum, near, part, cat,
    states, sother, grads, gother, g0other, tree, recv, dsend, drecv, dtree, psum,
    in_sem, s_send, s_recv, g_send, g_recv, f_send, f_recv, r_send, r_recv,
    b_send, b_recv, d_send, d_recv, p_send, p_recv,
    *, factor, scale,
):
    heads, length, _ = qb.shape
    tiles = length // SUB
    half = heads // 2
    me = lax.axis_index("ctx")
    z = lax.axis_index("heads")
    core = me % 2
    y = (me // 2) % 4
    x = me // 8
    mine = core * half
    theirs = (1 - core) * half
    sibling = me + 1 - 2 * core
    at = lambda px, py: (px * 4 + py) * 2 + core
    hops = (at(x, y + 1 - 2 * (y % 2)), at(x, 3 - y), at(x + 1 - 2 * (x % 2), y), at(3 - x, y))
    bits = (core == 1, y % 2 == 1, y // 2 == 1, x % 2 == 1, x // 2 == 1)

    def pick(level):
        return jnp.where(level == 0, hops[0], jnp.where(level == 1, hops[1], jnp.where(level == 2, hops[2], hops[3])))

    def remote(src, dst, send, got, device):
        return pltpu.make_async_remote_copy(
            src_ref=src, dst_ref=dst, send_sem=send, recv_sem=got, device_id=device, device_id_type=MESH
        )

    loads = ((kb, k_hbm), (vb, v_hbm), (qb, q_hbm), (gb, g_hbm))

    def load(n, h):
        return pltpu.make_async_copy(loads[n][1].at[h], loads[n][0].at[h], in_sem.at[n, h])

    def load_pair(n, h):
        load(n, h).start()
        load(n + 1, h).start()

    for n in (0, 2):
        for u in range(half):
            load_pair(n, theirs + u)
            load_pair(n, mine + u)

    barrier = pltpu.get_barrier_semaphore()
    for d in range(1, 4):
        pl.semaphore_signal(barrier, inc=1, device_id={"ctx": at(x, (y + d) % 4)}, device_id_type=MESH)
        pl.semaphore_signal(barrier, inc=1, device_id={"ctx": at((x + d) % 4, y)}, device_id_type=MESH)
    for d in range(1, 8):
        spot = (z * 2 + core + d) % 8
        device = {"ctx": me - core + spot % 2, "heads": spot // 2}
        pl.semaphore_signal(barrier, inc=1, device_id=device, device_id_type=MESH)

    def make_state(h):
        load(0, h).wait()
        load(1, h).wait()
        s = [mm(kb[h, pl.ds(c * SUB, SUB)], vb[h, pl.ds(c * SUB, SUB)], TN) for c in range(tiles)]
        pair = s[0] + s[1]
        near[h, 0] = s[0].astype(BF16)
        near[h, 1] = s[2].astype(BF16)
        near[h, 2] = pair.astype(BF16)
        states[h] = pair + (s[2] + s[3])

    def state_copy(u, low):
        block = states.at[low + u]
        return remote(block, sother.at[low + u], s_send.at[u], s_recv.at[u], {"ctx": sibling})

    def rest_copy(low):
        block = pl.ds(low, half)
        return remote(states.at[block], sother.at[block], s_send.at[half], s_recv.at[half], {"ctx": sibling})

    def make_grad(h):
        load(2, h).wait()
        load(3, h).wait()
        total = None
        for c in range(tiles):
            rows = pl.ds(c * SUB, SUB)
            wide_grad = gb[h, rows].astype(F32)
            scaled = jnp.concatenate([(wide[2 + j, rows] * wide_grad).astype(BF16) for j in range(5)], axis=1)
            value = mm(qb[h, rows], scaled, TN)
            total = value if total is None else total + value
        for j in range(5):
            grads[j, h] = jnp.where(bits[j], total[:, j * 128 : (j + 1) * 128], 0.0)

    def tree_copy(level, u):
        return remote(
            tree.at[level, u], recv.at[level, mine + u], f_send.at[level, u], f_recv.at[level, u], {"ctx": pick(level)}
        )

    def relay(level, u, low):
        block = recv.at[level, low + u]
        return remote(block, block, r_send.at[level, u], r_recv.at[level, u], {"ctx": sibling})

    def dtree_copy(level, u):
        return remote(
            dsend.at[level, u], drecv.at[level, u], b_send.at[level, u], b_recv.at[level, u], {"ctx": pick(level)}
        )

    def dtree_relay(u, low):
        block = dtree.at[low + u]
        return remote(block, block, d_send.at[u], d_recv.at[u], {"ctx": sibling})

    def grad_copy(u):
        return remote(grads.at[pl.ds(1, 4), theirs + u], gother.at[:, u], g_send.at[u], g_recv.at[u], {"ctx": sibling})

    def grad0_copy():
        return remote(grads.at[0], g0other, g_send.at[half], g_recv.at[half], {"ctx": sibling})

    def start_tree(u):
        state_copy(u, mine).wait_recv()
        tree[0, u] = states[mine + u] + sother[mine + u]
        tree_copy(0, u).start()

    def start_dtree(u):
        grad_copy(u).wait_recv()
        dsend[3, u] = grads[4, mine + u] + gother[3, u]
        dtree_copy(3, u).start()

    def tree_step(step):
        level = step // half
        u = step % half
        tree_copy(level, u).wait_recv()
        relay(level, u, mine).start()

        @pl.when(level < 3)
        def _():
            tree[level + 1, u] = tree[level, u] + recv[level, mine + u]
            tree_copy(level + 1, u).start()

    def dtree_step(step):
        level = step // half
        u = step % half
        back = 3 - level
        dtree_copy(back, u).wait_recv()

        @pl.when(level == 0)
        def _():
            dtree[mine + u] = drecv[back, u]

        @pl.when(level > 0)
        def _():
            dtree[mine + u] = dtree[mine + u] + drecv[back, u]

        @pl.when(level < 3)
        def _():
            dsend[back - 1, u] = dtree[mine + u] + (grads[back, mine + u] + gother[back - 1, u])
            dtree_copy(back - 1, u).start()

        @pl.when(level == 3)
        def _():
            dtree_relay(u, mine).start()

    def state_step(u, carry):
        make_state(theirs + u)

        @pl.when(u == 0)
        def _():
            pl.semaphore_wait(barrier, PARTNERS)

        state_copy(u, theirs).start()
        make_state(mine + u)

        @pl.when(u >= 2)
        def _():
            start_tree(u - 2)

        return carry

    lax.fori_loop(0, half, state_step, 0)
    rest_copy(mine).start()
    start_tree(2)
    wsum[...] = jnp.zeros_like(wsum)
    lsum[...] = jnp.zeros_like(lsum)
    start_tree(3)
    hot = one_hot(index_ref[...], table_ref.shape[1])
    fill_lambda(hot, table_ref, wide, diag, factor)

    def grad_step(u, carry):
        make_grad(theirs + u)
        grad_copy(u).start()
        make_grad(mine + u)

        @pl.when(u >= 1)
        def _():
            start_dtree(u - 1)

        tree_step(u)
        return carry

    lax.fori_loop(0, half, grad_step, 0)
    grad0_copy().start()
    start_dtree(3)

    def local_head(h, between):
        def tile(c):
            rows = pl.ds(c * SUB, SUB)
            return rows, qb[h, rows], kb[h, rows], vb[h, rows], gb[h, rows]

        near_grad = {}
        pair_grad = None
        for c in range(tiles - 1, -1, -1):
            if c == 1:
                between()
            rows, q, k, v, grad = tile(c)
            score = mm(q, k, NT)
            back = mm(grad, v, NT)
            wsum[c] += score * back
            weight = diag[c]
            weighted = (weight * score).astype(BF16)
            dscore = (weight * back).astype(BF16)
            out = mm(weighted, v, NN)
            qg = mm(dscore, k, NN)
            kg = mm(dscore, q, TN)
            vg = mm(weighted, grad, TN)
            use = ([0] if c % 2 else []) + ([1] if c >= 2 else [])
            if use:
                buckets = ([near[h, c // 2]] if c % 2 else []) + ([near[h, 2]] if c >= 2 else [])
                joined = jnp.concatenate(buckets, axis=1)
                cross = mm(q, joined, NN)
                wide_grad = grad.astype(F32)
                scaled = []
                for n, level in enumerate(use):
                    piece = cross[:, n * 128 : (n + 1) * 128]
                    lam = wide[level, rows]
                    out += lam * piece
                    lsum[level, rows] += piece * wide_grad
                    scaled.append((lam * wide_grad).astype(BF16))
                scaled = jnp.concatenate(scaled, axis=1)
                qg += mm(scaled, joined, NT)
                value = mm(q, scaled, TN)
                for n, level in enumerate(use):
                    piece = value[:, n * 128 : (n + 1) * 128]
                    if level == 0:
                        near_grad[c - 1] = piece
                    else:
                        pair_grad = piece if pair_grad is None else pair_grad + piece
            dstate = near_grad.get(c)
            if c < 2:
                dstate = pair_grad if dstate is None else dstate + pair_grad
            if dstate is not None:
                dlocal[c] = dstate
            lout[h, rows] = out
            lq[h, rows] = qg
            lk[h, rows] = kg
            lv[h, rows] = vg
        return dlocal

    dlocal = {}

    def local_step(h, carry):
        def comm_step(step):
            @pl.when((step >= TREE_LAG) & (step < TREE_LAG + 3 * half))
            def _():
                tree_step(step - TREE_LAG + half)

            @pl.when(step >= half)
            def _():
                dtree_step(step - half)

        local_head(h, lambda: comm_step(2 * h))
        for c in range(3):
            part[h, c] = dlocal[c]
        comm_step(2 * h + 1)
        return carry

    lax.fori_loop(0, heads, local_step, 0)

    lane = lax.broadcasted_iota(jnp.int32, (table_ref.shape[1], 128), 1)
    hot = one_hot(index_ref[...], table_ref.shape[1])
    rows_id = lax.broadcasted_iota(jnp.int32, (SUB, SUB), 0)
    cols_id = lax.broadcasted_iota(jnp.int32, (SUB, SUB), 1)
    crossed = jnp.bitwise_xor(rows_id, cols_id)
    table = jnp.zeros(lane.shape, F32)
    for level in range(11):
        if level < 9:
            low = (1 << (level - 1)) if level else 0
            mask = (crossed >= low) & (crossed < (1 << level)) & (cols_id <= rows_id)
            values = []
            for c in range(tiles):
                value = jnp.where(mask, wsum[c], 0.0)
                values.append(value[:, :128] + value[:, 128:])
            value = jnp.concatenate(values, axis=0)
        else:
            value = lsum[level - 9]
        table = jnp.where(lane == level, row_sums(hot, value), table)

    rest_copy(theirs).wait_recv()
    for level in range(4):
        for u in range(half):
            relay(level, u, theirs).wait_recv()

    def cross_step(h, carry):
        cat[h, :, 0:128] = jnp.where(bits[0], sother[h], 0.0).astype(BF16)
        for j in range(1, 5):
            cat[h, :, j * 128 : (j + 1) * 128] = jnp.where(bits[j], recv[j - 1, h], 0.0).astype(BF16)
        joined = cat[h]
        for c in range(tiles):
            rows = pl.ds(c * SUB, SUB)
            cross = mm(qb[h, rows], joined, NN)
            wide_grad = gb[h, rows].astype(F32)
            out = lout[h, rows]
            for j in range(5):
                piece = cross[:, j * 128 : (j + 1) * 128]
                out += wide[2 + j, rows] * piece
                lsum[2 + j, rows] += piece * wide_grad
            out_ref[h, rows] = out.astype(BF16)

        @pl.when(h % 2 == 1)
        def _():
            dtree_step(3 * half + h // 2)

        return carry

    lax.fori_loop(0, heads, cross_step, 0)
    for level in range(11, 16):
        table = jnp.where(lane == level, row_sums(hot, lsum[level - 9]), table)

    spots = (z * 2 + core, y, x)
    sizes = (8, 4, 4)
    psum[0, spots[0]] = (table * scale).T[0:16]

    def table_copy(phase, d):
        other = (spots[phase] + d) % sizes[phase]
        device = (
            {"ctx": at(x, y) - core + other % 2, "heads": other // 2},
            {"ctx": at(x, other)},
            {"ctx": at(other, y)},
        )[phase]
        slot = psum.at[phase, spots[phase]]
        return remote(slot, slot, p_send.at[phase, d - 1], p_recv.at[phase, d - 1], device)

    def table_wait(phase, d):
        other = (spots[phase] + sizes[phase] - d) % sizes[phase]
        slot = psum.at[phase, other]
        return remote(slot, slot, p_send.at[phase, d - 1], p_recv.at[phase, d - 1], {"ctx": sibling})

    for d in range(1, 8):
        table_copy(0, d).start()

    def table_phase(phase):
        for d in range(1, sizes[phase]):
            table_wait(phase, d).wait_recv()
        value = psum[phase, 0]
        for n in range(1, sizes[phase]):
            value = value + psum[phase, n]
        if phase < 2:
            psum[phase + 1, spots[phase + 1]] = value
            for d in range(1, 4):
                table_copy(phase + 1, d).start()
        else:
            total_ref[...] = value[:, 0:64]

    for u in range(half):
        dtree_relay(u, theirs).wait_recv()
    grad0_copy().wait_recv()

    def grad_head(h):
        joined = cat[h]
        far = dtree[h] + jnp.where(bits[0], 0.0, g0other[h])
        for c in range(tiles):
            rows = pl.ds(c * SUB, SUB)
            wide_grad = gb[h, rows].astype(F32)
            scaled = jnp.concatenate([(wide[2 + j, rows] * wide_grad).astype(BF16) for j in range(5)], axis=1)
            qg = lq[h, rows] + mm(scaled, joined, NT)
            dstate = (far + part[h, c] if c < 3 else far).astype(BF16)
            kg = lk[h, rows] + mm(vb[h, rows], dstate, NT)
            vg = lv[h, rows] + mm(kb[h, rows], dstate, NN)
            qg_ref[h, rows] = qg.astype(BF16)
            kg_ref[h, rows] = kg.astype(BF16)
            vg_ref[h, rows] = vg.astype(BF16)

    def grad_loop(low, high):
        def step(h, carry):
            grad_head(h)
            return carry

        lax.fori_loop(low, high, step, 0)

    grad_loop(0, 3)
    table_phase(0)
    grad_loop(3, 6)
    table_phase(1)
    grad_loop(6, heads)
    table_phase(2)

    rest_copy(mine).wait_send()
    grad0_copy().wait_send()
    for u in range(half):
        state_copy(u, theirs).wait_send()
        grad_copy(u).wait_send()
        for level in range(4):
            tree_copy(level, u).wait_send()
            relay(level, u, mine).wait_send()
            dtree_copy(level, u).wait_send()
        dtree_relay(u, mine).wait_send()
    for phase in range(3):
        for d in range(1, sizes[phase]):
            table_copy(phase, d).wait_send()


def put_kernel(*refs):
    sems = refs[-1]
    count = (len(refs) - 1) // 2
    copies = []
    for n in range(count - 1):
        for h in range(0, refs[n].shape[0], 2):
            rows = pl.ds(h, 2)
            copies.append((refs[n].at[rows], refs[count + n].at[rows]))
    copies.append((refs[count - 1], refs[2 * count - 1]))
    copies = [pltpu.make_async_copy(src, dst, sems.at[i]) for i, (src, dst) in enumerate(copies)]
    for copy in copies:
        copy.start()
    for copy in copies:
        copy.wait()


def body(queries, keys, values, out_grad, level_table, table_index):
    heads, length, width = queries.shape
    devices = lax.axis_size("ctx")
    factor = 1.0 / math.sqrt(width * length * devices)
    tiles = length // SUB
    half = heads // 2
    dma = lambda *shape: pltpu.SemaphoreType.DMA(shape)
    square = (width, width)
    table_lanes = level_table.shape[0]
    outs = pl.pallas_call(
        functools.partial(kernel, factor=factor, scale=factor / math.sqrt(length * devices)),
        out_shape=tuple(pltpu.VMEM(queries.shape, BF16) for _ in range(4))
        + (pltpu.VMEM(level_table.shape[::-1], F32),),
        in_specs=[pl.BlockSpec(memory_space=pltpu.HBM)] * 4 + [pl.BlockSpec(memory_space=pltpu.VMEM)] * 2,
        out_specs=(pl.BlockSpec(memory_space=pltpu.VMEM),) * 5,
        scratch_shapes=[pltpu.VMEM(queries.shape, BF16)] * 4
        + [pltpu.VMEM(queries.shape, F32)] * 4
        + [
            pltpu.VMEM((7, length, 128), F32),
            pltpu.VMEM((tiles, SUB, SUB), F32),
            pltpu.VMEM((tiles, SUB, SUB), F32),
            pltpu.VMEM((7, length, 128), F32),
            pltpu.VMEM((heads, 3) + square, BF16),
            pltpu.VMEM((heads, 3) + square, F32),
            pltpu.VMEM((heads, width, 5 * width), BF16),
            pltpu.VMEM((heads,) + square, F32),
            pltpu.VMEM((heads,) + square, F32),
            pltpu.VMEM((5, heads) + square, F32),
            pltpu.VMEM((4, half) + square, F32),
            pltpu.VMEM((heads,) + square, F32),
            pltpu.VMEM((4, half) + square, F32),
            pltpu.VMEM((4, heads) + square, F32),
            pltpu.VMEM((4, half) + square, F32),
            pltpu.VMEM((4, half) + square, F32),
            pltpu.VMEM((heads,) + square, F32),
            pltpu.VMEM((3, 8, 16, table_lanes), F32),
            dma(4, heads), dma(half + 1), dma(half + 1), dma(half + 1), dma(half + 1),
            dma(4, half), dma(4, half), dma(4, half), dma(4, half),
            dma(4, half), dma(4, half), dma(half), dma(half), dma(3, 7), dma(3, 7),
        ],
        compiler_params=pltpu.CompilerParams(
            collective_id=0, has_side_effects=True, vmem_limit_bytes=52 << 20
        ),
    )(queries, keys, values, out_grad, table_index.reshape(1, length), level_table.T)
    outs = pl.pallas_call(
        put_kernel,
        out_shape=tuple(jax.ShapeDtypeStruct(queries.shape, BF16) for _ in range(4))
        + (jax.ShapeDtypeStruct(level_table.shape[::-1], F32),),
        in_specs=[pl.BlockSpec(memory_space=pltpu.VMEM)] * 5,
        out_specs=(pl.BlockSpec(memory_space=pltpu.HBM),) * 5,
        scratch_shapes=[dma(4 * heads // 2 + 1)],
        compiler_params=pltpu.CompilerParams(vmem_limit_bytes=1 << 20),
    )(*[pltpu.with_memory_space_constraint(value, pltpu.VMEM) for value in outs])
    return outs[:4] + (outs[4].T,)


def solution(mesh):
    placed = (P("heads", "ctx", None),) * 4
    return jax.shard_map(
        body,
        mesh=mesh,
        in_specs=placed + (P(), P("ctx")),
        out_specs=placed + (P(),),
        check_vma=False,
    )
```

```python
import functools
import math

import jax
import jax.numpy as jnp
from jax import lax
from jax.experimental import pallas as pl
from jax.experimental.pallas import tpu as pltpu
from jax.sharding import PartitionSpec as P

SUB = 256
PARTNERS = 22
TREE_LAG = 1
DTREE_LAG = 4
MESH = pl.DeviceIdType.MESH
F32 = jnp.float32
BF16 = jnp.bfloat16
NN = (((1,), (0,)), ((), ()))
NT = (((1,), (1,)), ((), ()))
TN = (((0,), (0,)), ((), ()))
TT = (((0,), (1,)), ((), ()))


def mm(a, b, dims):
    return lax.dot_general(a, b, dims, preferred_element_type=F32)


def split3(value):
    first = value.astype(BF16)
    rest = value - first.astype(F32)
    second = rest.astype(BF16)
    third = (rest - second.astype(F32)).astype(BF16)
    return first, second, third


def one_hot(index_row, rows):
    length = index_row.shape[1]
    row_ids = lax.broadcasted_iota(jnp.int32, (rows, length), 0)
    return jnp.where(row_ids == index_row, 1.0, 0.0).astype(BF16)


def fill_lambda(hot, table_ref, wide_ref, diag_ref, factor):
    table = (table_ref[...] * factor).T
    hots = jnp.concatenate([hot, hot], axis=0)
    length = hot.shape[1]

    def wide_lams(level):
        columns = jnp.concatenate(
            [jnp.broadcast_to(table[:, n : n + 1], (table.shape[0], 128)) for n in (level, level + 1)], axis=1
        )
        value = mm(hots, jnp.concatenate(split3(columns)[:2], axis=0), TN)
        return value[:, :128], value[:, 128:]

    lams = [lam for level in range(0, 16, 2) for lam in wide_lams(level)]
    for level in range(wide_ref.shape[0]):
        wide_ref[level] = lams[9 + level]
    rows = lax.broadcasted_iota(jnp.int32, (128, 128), 0)
    cols = lax.broadcasted_iota(jnp.int32, (128, 128), 1)
    crossed = jnp.bitwise_xor(rows, cols)
    for level in range(8):
        lam = lams[level]
        for n in range(length // 128):
            tile, half = n // 2, n % 2
            spot = pl.ds(half * 128, 128)
            part = lam[n * 128 : (n + 1) * 128]
            if level == 0:
                diag_ref[tile, spot, spot] = jnp.where(cols <= rows, part, 0.0)
            else:
                low = 1 << (level - 1)
                diag_ref[tile, spot, spot] = jnp.where(
                    (crossed >= low) & (cols <= rows), part, diag_ref[tile, spot, spot]
                )
    lam = lams[8]
    for tile in range(length // SUB):
        diag_ref[tile, 0:128, 128:256] = jnp.zeros((128, 128), F32)
        diag_ref[tile, 128:256, 0:128] = lam[tile * SUB + 128 : (tile + 1) * SUB]


def row_sums(hot, value):
    high, rest, _ = split3(value)
    total = mm(hot, high, NN) + mm(hot, rest, NN)
    return jnp.sum(total, axis=1, keepdims=True)


def kernel(
    q_hbm, k_hbm, v_hbm, g_hbm, index_ref, table_ref,
    out_ref, qg_ref, kg_ref, vg_ref, total_ref,
    qb, kb, vb, gb, lout, lq, lk, lv, wide, diag, wsum, lsum, near, part, stack, pa, da, pb, db,
    states, sother, grads, gother, g0other, tree, recv, dsend, drecv, dtree, psum,
    in_sem, s_send, s_recv, g_send, g_recv, f_send, f_recv, r_send, r_recv,
    b_send, b_recv, d_send, d_recv, p_send, p_recv,
    *, factor, scale,
):
    heads, length, _ = qb.shape
    tiles = length // SUB
    half = heads // 2
    me = lax.axis_index("ctx")
    z = lax.axis_index("heads")
    core = me % 2
    y = (me // 2) % 4
    x = me // 8
    mine = core * half
    theirs = (1 - core) * half
    sibling = me + 1 - 2 * core
    at = lambda px, py: (px * 4 + py) * 2 + core
    hops = (at(x, y + 1 - 2 * (y % 2)), at(x, 3 - y), at(x + 1 - 2 * (x % 2), y), at(3 - x, y))
    bits = (core == 1, y % 2 == 1, y // 2 == 1, x % 2 == 1, x // 2 == 1)

    def pick(level):
        return jnp.where(level == 0, hops[0], jnp.where(level == 1, hops[1], jnp.where(level == 2, hops[2], hops[3])))

    def remote(src, dst, send, got, device):
        return pltpu.make_async_remote_copy(
            src_ref=src, dst_ref=dst, send_sem=send, recv_sem=got, device_id=device, device_id_type=MESH
        )

    loads = ((kb, k_hbm), (vb, v_hbm), (qb, q_hbm), (gb, g_hbm))

    def load(n, h):
        return pltpu.make_async_copy(loads[n][1].at[h], loads[n][0].at[h], in_sem.at[n, h])

    def load_pair(n, h):
        load(n, h).start()
        load(n + 1, h).start()

    for n in (0, 2):
        for u in range(half):
            load_pair(n, theirs + u)
            load_pair(n, mine + u)

    barrier = pltpu.get_barrier_semaphore()
    for d in range(1, 16):
        spot = (x * 4 + y + d) % 16
        pl.semaphore_signal(barrier, inc=1, device_id={"ctx": at(spot // 4, spot % 4)}, device_id_type=MESH)
    for d in range(1, 8):
        spot = (z * 2 + core + d) % 8
        device = {"ctx": me - core + spot % 2, "heads": spot // 2}
        pl.semaphore_signal(barrier, inc=1, device_id=device, device_id_type=MESH)

    def make_state(h):
        load(0, h).wait()
        load(1, h).wait()
        s = [mm(kb[h, pl.ds(c * SUB, SUB)], vb[h, pl.ds(c * SUB, SUB)], TN) for c in range(tiles)]
        pair = s[0] + s[1]
        near[h, 0] = s[0].astype(BF16)
        near[h, 1] = s[2].astype(BF16)
        near[h, 2] = pair.astype(BF16)
        states[h] = pair + (s[2] + s[3])

    def state_copy(u, low):
        block = states.at[low + u]
        return remote(block, sother.at[low + u], s_send.at[u], s_recv.at[u], {"ctx": sibling})

    def rest_copy(low):
        block = pl.ds(low, half)
        return remote(states.at[block], sother.at[block], s_send.at[half], s_recv.at[half], {"ctx": sibling})

    def make_grad(h, low, high):
        total = None
        for c in range(tiles):
            rows = pl.ds(c * SUB, SUB)
            wide_grad = gb[h, rows].astype(F32)
            scaled = jnp.concatenate([(wide[2 + j, rows] * wide_grad).astype(BF16) for j in range(low, high)], axis=1)
            value = mm(qb[h, rows], scaled, TN)
            total = value if total is None else total + value
        for j in range(low, high):
            grads[j, h] = jnp.where(bits[j], total[:, (j - low) * 128 : (j - low + 1) * 128], 0.0)

    def tree_copy(level, u):
        return remote(
            tree.at[level, u], recv.at[level, mine + u], f_send.at[level, u], f_recv.at[level, u], {"ctx": pick(level)}
        )

    def relay(level, u, low):
        block = recv.at[level, low + u]
        return remote(block, block, r_send.at[level, u], r_recv.at[level, u], {"ctx": sibling})

    def dtree_copy(level, u):
        return remote(
            dsend.at[level, u], drecv.at[level, u], b_send.at[level, u], b_recv.at[level, u], {"ctx": pick(level)}
        )

    def dtree_relay(u, low):
        block = dtree.at[low + u]
        return remote(block, block, d_send.at[u], d_recv.at[u], {"ctx": sibling})

    def grad_copy(u, low):
        return remote(
            grads.at[pl.ds(low, 2), theirs + u], gother.at[pl.ds(low - 1, 2), u],
            g_send.at[low // 2, u], g_recv.at[low // 2, u], {"ctx": sibling},
        )

    def grad0_copy():
        return remote(grads.at[0], g0other, g_send.at[2, 0], g_recv.at[2, 0], {"ctx": sibling})

    def start_tree(u):
        state_copy(u, mine).wait_recv()
        tree[0, u] = states[mine + u] + sother[mine + u]
        tree_copy(0, u).start()

    def start_dtree(u):
        grad_copy(u, 3).wait_recv()
        dsend[3, u] = grads[4, mine + u] + gother[3, u]
        dtree_copy(3, u).start()

    def tree_step(step):
        level = step // half
        u = step % half
        tree_copy(level, u).wait_recv()
        relay(level, u, mine).start()

        @pl.when(level < 3)
        def _():
            tree[level + 1, u] = tree[level, u] + recv[level, mine + u]
            tree_copy(level + 1, u).start()

    def dtree_step(step):
        level = step // half
        u = step % half
        back = 3 - level
        dtree_copy(back, u).wait_recv()

        @pl.when(level == 0)
        def _():
            dtree[mine + u] = drecv[back, u]

        @pl.when(level > 0)
        def _():
            dtree[mine + u] = dtree[mine + u] + drecv[back, u]

        @pl.when(level == 1)
        def _():
            grad_copy(u, 1).wait_recv()

        @pl.when(level < 3)
        def _():
            dsend[back - 1, u] = dtree[mine + u] + (grads[back, mine + u] + gother[back - 1, u])
            dtree_copy(back - 1, u).start()

        @pl.when(level == 3)
        def _():
            dtree_relay(u, mine).start()

    def state_step(u, carry):
        make_state(theirs + u)

        @pl.when(u == 0)
        def _():
            pl.semaphore_wait(barrier, PARTNERS)

        state_copy(u, theirs).start()
        make_state(mine + u)

        @pl.when(u >= 2)
        def _():
            start_tree(u - 2)

        return carry

    lax.fori_loop(0, half, state_step, 0)
    rest_copy(mine).start()
    start_tree(2)
    wsum[...] = jnp.zeros_like(wsum)
    lsum[...] = jnp.zeros_like(lsum)
    start_tree(3)
    hot = one_hot(index_ref[...], table_ref.shape[1])
    fill_lambda(hot, table_ref, wide, diag, factor)

    def grad_step(u, carry):
        load(2, theirs + u).wait()
        load(3, theirs + u).wait()
        make_grad(theirs + u, 0, 5)
        grad_copy(u, 3).start()
        grad_copy(u, 1).start()
        load(2, mine + u).wait()
        load(3, mine + u).wait()
        make_grad(mine + u, 0, 5)

        @pl.when(u >= 1)
        def _():
            start_dtree(u - 1)

        tree_step(u)
        return carry

    lax.fori_loop(0, half, grad_step, 0)
    grad0_copy().start()
    start_dtree(3)

    def tile_of(h, c):
        rows = pl.ds(c * SUB, SUB)
        return rows, qb[h, rows], kb[h, rows], vb[h, rows], gb[h, rows]

    def score_head(h, weighted, dscore):
        for c in range(tiles):
            rows, q, k, v, grad = tile_of(h, c)
            score = mm(q, k, NT)
            back = mm(grad, v, NT)
            wsum[c] += score * back
            weight = diag[c]
            weighted[c] = (weight * score).astype(BF16)
            dscore[c] = (weight * back).astype(BF16)

    def local_head(h, weighted, dscore):
        near_grad = {}
        pair_grad = None
        for c in range(tiles - 1, -1, -1):
            rows, q, k, v, grad = tile_of(h, c)
            out = mm(weighted[c], v, NN)
            qg = mm(dscore[c], k, NN)
            kg = mm(dscore[c], q, TN)
            vg = mm(weighted[c], grad, TN)
            use = ([0] if c % 2 else []) + ([1] if c >= 2 else [])
            if use:
                buckets = ([near[h, c // 2]] if c % 2 else []) + ([near[h, 2]] if c >= 2 else [])
                joined = jnp.concatenate(buckets, axis=1)
                cross = mm(q, joined, NN)
                wide_grad = grad.astype(F32)
                scaled = []
                for n, level in enumerate(use):
                    piece = cross[:, n * 128 : (n + 1) * 128]
                    lam = wide[level, rows]
                    out += lam * piece
                    lsum[level, rows] += piece * wide_grad
                    scaled.append((lam * wide_grad).astype(BF16))
                scaled = jnp.concatenate(scaled, axis=1)
                qg += mm(scaled, joined, NT)
                value = mm(q, scaled, TN)
                for n, level in enumerate(use):
                    piece = value[:, n * 128 : (n + 1) * 128]
                    if level == 0:
                        near_grad[c - 1] = piece
                    else:
                        pair_grad = piece if pair_grad is None else pair_grad + piece
            dstate = near_grad.get(c)
            if c < 2:
                dstate = pair_grad if dstate is None else dstate + pair_grad
            if dstate is not None:
                part[h, c] = dstate
            lout[h, rows] = out
            lq[h, rows] = qg
            lk[h, rows] = kg
            lv[h, rows] = vg

    def comm_step(step):
        @pl.when((step >= TREE_LAG) & (step < TREE_LAG + 3 * half))
        def _():
            tree_step(step - TREE_LAG + half)

        @pl.when(step >= DTREE_LAG)
        def _():
            dtree_step(step - DTREE_LAG)

    def local_step(i, carry):
        h = 2 * i
        local_head(h, pa, da)
        score_head(h + 1, pb, db)
        comm_step(2 * h)
        comm_step(2 * h + 1)
        local_head(h + 1, pb, db)
        score_head(h + 2, pa, da)
        comm_step(2 * h + 2)
        comm_step(2 * h + 3)
        return carry

    score_head(0, pa, da)
    lax.fori_loop(0, heads // 2 - 1, local_step, 0)
    local_head(heads - 2, pa, da)
    score_head(heads - 1, pb, db)
    comm_step(2 * heads - 4)
    comm_step(2 * heads - 3)
    local_head(heads - 1, pb, db)
    comm_step(2 * heads - 2)
    comm_step(2 * heads - 1)

    lane = lax.broadcasted_iota(jnp.int32, (table_ref.shape[1], 128), 1)
    hot = one_hot(index_ref[...], table_ref.shape[1])
    rows_id = lax.broadcasted_iota(jnp.int32, (128, 128), 0)
    cols_id = lax.broadcasted_iota(jnp.int32, (128, 128), 1)
    crossed = jnp.bitwise_xor(rows_id, cols_id)
    table = jnp.zeros(lane.shape, F32)
    blocks = [wsum[n // 2, (n % 2) * 128 : (n % 2 + 1) * 128, (n % 2) * 128 : (n % 2 + 1) * 128] for n in range(2 * tiles)]
    high, rest, _ = split3(jnp.concatenate(blocks, axis=0))
    for level in range(8):
        low = (1 << (level - 1)) if level else 0
        mask = (crossed >= low) & (crossed < (1 << level)) & (cols_id <= rows_id)
        mask = jnp.where(mask, 1.0, 0.0).astype(BF16)
        mask = jnp.concatenate([mask] * (2 * tiles), axis=0)
        total = mm(hot, high * mask, NN) + mm(hot, rest * mask, NN)
        table = jnp.where(lane == level, jnp.sum(total, axis=1, keepdims=True), table)
    lower = [wsum[c, 128:256, 0:128] for c in range(tiles)]
    clear = jnp.zeros((128, 128), F32)
    lower = jnp.concatenate([piece for block in lower for piece in (clear, block)], axis=0)
    table = jnp.where(lane == 8, row_sums(hot, lower), table)
    for level in range(9, 11):
        table = jnp.where(lane == level, row_sums(hot, lsum[level - 9]), table)

    rest_copy(theirs).wait_recv()
    for level in range(4):
        for u in range(half):
            relay(level, u, theirs).wait_recv()

    def lam_step(h, carry):
        buckets = [jnp.where(bits[0], sother[h], 0.0).astype(BF16)]
        for j in range(1, 5):
            buckets.append(jnp.where(bits[j], recv[j - 1, h], 0.0).astype(BF16))
        stack[h] = jnp.concatenate(buckets, axis=0)
        joined = jnp.concatenate(buckets, axis=1)
        for c in range(tiles):
            rows = pl.ds(c * SUB, SUB)
            cross = mm(qb[h, rows], joined, NN)
            wide_grad = gb[h, rows].astype(F32)
            for j in range(5):
                lsum[2 + j, rows] += cross[:, j * 128 : (j + 1) * 128] * wide_grad
        return carry

    lax.fori_loop(0, heads, lam_step, 0)
    for level in range(11, 16):
        table = jnp.where(lane == level, row_sums(hot, lsum[level - 9]), table)

    spots = (z * 2 + core, x * 4 + y)
    sizes = (8, 16)
    psum[0, spots[0]] = (table * scale).T[0:16]

    def table_copy(phase, d):
        other = (spots[phase] + d) % sizes[phase]
        device = (
            {"ctx": me - core + other % 2, "heads": other // 2},
            {"ctx": at(other // 4, other % 4)},
        )[phase]
        slot = psum.at[phase, spots[phase]]
        return remote(slot, slot, p_send.at[phase, d - 1], p_recv.at[phase, d - 1], device)

    def table_wait(phase, d):
        other = (spots[phase] + sizes[phase] - d) % sizes[phase]
        slot = psum.at[phase, other]
        return remote(slot, slot, p_send.at[phase, d - 1], p_recv.at[phase, d - 1], {"ctx": sibling})

    for d in range(1, 8):
        table_copy(0, d).start()

    def table_phase(phase):
        for d in range(1, sizes[phase]):
            table_wait(phase, d).wait_recv()
        value = psum[phase, 0]
        for n in range(1, sizes[phase]):
            value = value + psum[phase, n]
        if phase < 1:
            psum[1, spots[1]] = value
            for d in range(1, 16):
                table_copy(1, d).start()
        else:
            total_ref[...] = value[:, 0:64]

    def out_step(h, carry):
        joined = jnp.concatenate([stack[h, j * 128 : (j + 1) * 128] for j in range(5)], axis=1)
        for c in range(tiles):
            rows = pl.ds(c * SUB, SUB)
            cross = mm(qb[h, rows], joined, NN)
            out = lout[h, rows]
            for j in range(5):
                out += wide[2 + j, rows] * cross[:, j * 128 : (j + 1) * 128]
            out_ref[h, rows] = out.astype(BF16)

        @pl.when(h < DTREE_LAG)
        def _():
            dtree_step(4 * half - DTREE_LAG + h)

        return carry

    lax.fori_loop(0, heads, out_step, 0)
    table_phase(0)
    for u in range(half):
        dtree_relay(u, theirs).wait_recv()
    grad0_copy().wait_recv()

    def grad_head(h):
        joined = stack[h]
        far = dtree[h] + jnp.where(bits[0], 0.0, g0other[h])
        for c in range(tiles):
            rows = pl.ds(c * SUB, SUB)
            back = mm(gb[h, rows], joined, NT)
            qg = lq[h, rows]
            for j in range(5):
                qg += wide[2 + j, rows] * back[:, j * 128 : (j + 1) * 128]
            dstate = (far + part[h, c] if c < 3 else far).astype(BF16)
            kg = lk[h, rows] + mm(vb[h, rows], dstate, NT)
            vg = lv[h, rows] + mm(kb[h, rows], dstate, NN)
            qg_ref[h, rows] = qg.astype(BF16)
            kg_ref[h, rows] = kg.astype(BF16)
            vg_ref[h, rows] = vg.astype(BF16)

    def grad_loop(low, high):
        def step(h, carry):
            grad_head(h)
            return carry

        lax.fori_loop(low, high, step, 0)

    grad_loop(0, heads)
    table_phase(1)

    rest_copy(mine).wait_send()
    grad0_copy().wait_send()
    for u in range(half):
        state_copy(u, theirs).wait_send()
        grad_copy(u, 1).wait_send()
        grad_copy(u, 3).wait_send()
        for level in range(4):
            tree_copy(level, u).wait_send()
            relay(level, u, mine).wait_send()
            dtree_copy(level, u).wait_send()
        dtree_relay(u, mine).wait_send()
    for phase in range(2):
        for d in range(1, sizes[phase]):
            table_copy(phase, d).wait_send()


def put_kernel(*refs):
    sems = refs[-1]
    count = (len(refs) - 1) // 2
    copies = []
    for n in range(count - 1):
        for h in range(0, refs[n].shape[0], 2):
            rows = pl.ds(h, 2)
            copies.append((refs[n].at[rows], refs[count + n].at[rows]))
    copies.append((refs[count - 1], refs[2 * count - 1]))
    copies = [pltpu.make_async_copy(src, dst, sems.at[i]) for i, (src, dst) in enumerate(copies)]
    for copy in copies:
        copy.start()
    for copy in copies:
        copy.wait()


def body(queries, keys, values, out_grad, level_table, table_index):
    heads, length, width = queries.shape
    devices = lax.axis_size("ctx")
    factor = 1.0 / math.sqrt(width * length * devices)
    tiles = length // SUB
    half = heads // 2
    dma = lambda *shape: pltpu.SemaphoreType.DMA(shape)
    square = (width, width)
    table_lanes = level_table.shape[0]
    outs = pl.pallas_call(
        functools.partial(kernel, factor=factor, scale=factor / math.sqrt(length * devices)),
        out_shape=tuple(pltpu.VMEM(queries.shape, BF16) for _ in range(4))
        + (pltpu.VMEM(level_table.shape[::-1], F32),),
        in_specs=[pl.BlockSpec(memory_space=pltpu.HBM)] * 4 + [pl.BlockSpec(memory_space=pltpu.VMEM)] * 2,
        out_specs=(pl.BlockSpec(memory_space=pltpu.VMEM),) * 5,
        scratch_shapes=[pltpu.VMEM(queries.shape, BF16)] * 4
        + [pltpu.VMEM(queries.shape, F32)] * 4
        + [
            pltpu.VMEM((7, length, 128), F32),
            pltpu.VMEM((tiles, SUB, SUB), F32),
            pltpu.VMEM((tiles, SUB, SUB), F32),
            pltpu.VMEM((7, length, 128), F32),
            pltpu.VMEM((heads, 3) + square, BF16),
            pltpu.VMEM((heads, 3) + square, F32),
            pltpu.VMEM((heads, 5 * width, width), BF16),
            pltpu.VMEM((tiles, SUB, SUB), BF16),
            pltpu.VMEM((tiles, SUB, SUB), BF16),
            pltpu.VMEM((tiles, SUB, SUB), BF16),
            pltpu.VMEM((tiles, SUB, SUB), BF16),
            pltpu.VMEM((heads,) + square, F32),
            pltpu.VMEM((heads,) + square, F32),
            pltpu.VMEM((5, heads) + square, F32),
            pltpu.VMEM((4, half) + square, F32),
            pltpu.VMEM((heads,) + square, F32),
            pltpu.VMEM((4, half) + square, F32),
            pltpu.VMEM((4, heads) + square, F32),
            pltpu.VMEM((4, half) + square, F32),
            pltpu.VMEM((4, half) + square, F32),
            pltpu.VMEM((heads,) + square, F32),
            pltpu.VMEM((2, 16, 16, table_lanes), F32),
            dma(4, heads), dma(half + 1), dma(half + 1), dma(3, half), dma(3, half),
            dma(4, half), dma(4, half), dma(4, half), dma(4, half),
            dma(4, half), dma(4, half), dma(half), dma(half), dma(2, 15), dma(2, 15),
        ],
        compiler_params=pltpu.CompilerParams(
            collective_id=0, has_side_effects=True, vmem_limit_bytes=54 << 20
        ),
    )(queries, keys, values, out_grad, table_index.reshape(1, length), level_table.T)
    outs = pl.pallas_call(
        put_kernel,
        out_shape=tuple(jax.ShapeDtypeStruct(queries.shape, BF16) for _ in range(4))
        + (jax.ShapeDtypeStruct(level_table.shape[::-1], F32),),
        in_specs=[pl.BlockSpec(memory_space=pltpu.VMEM)] * 5,
        out_specs=(pl.BlockSpec(memory_space=pltpu.HBM),) * 5,
        scratch_shapes=[dma(4 * heads // 2 + 1)],
        compiler_params=pltpu.CompilerParams(vmem_limit_bytes=1 << 20),
    )(*[pltpu.with_memory_space_constraint(value, pltpu.VMEM) for value in outs])
    return outs[:4] + (outs[4].T,)


def solution(mesh):
    placed = (P("heads", "ctx", None),) * 4
    return jax.shard_map(
        body,
        mesh=mesh,
        in_specs=placed + (P(), P("ctx")),
        out_specs=placed + (P(),),
        check_vma=False,
    )
```

```python
import functools
import math

import jax
import jax.numpy as jnp
from jax import lax
from jax.experimental import pallas as pl
from jax.experimental.pallas import tpu as pltpu
from jax.sharding import PartitionSpec as P

SUB = 256
PARTNERS = 22
TREE_LAG = 0
DTREE_LAG = 4
MESH = pl.DeviceIdType.MESH
F32 = jnp.float32
BF16 = jnp.bfloat16
NN = (((1,), (0,)), ((), ()))
NT = (((1,), (1,)), ((), ()))
TN = (((0,), (0,)), ((), ()))
TT = (((0,), (1,)), ((), ()))


def mm(a, b, dims):
    return lax.dot_general(a, b, dims, preferred_element_type=F32)


def split3(value):
    first = value.astype(BF16)
    rest = value - first.astype(F32)
    second = rest.astype(BF16)
    third = (rest - second.astype(F32)).astype(BF16)
    return first, second, third


def one_hot(index_row, rows):
    length = index_row.shape[1]
    row_ids = lax.broadcasted_iota(jnp.int32, (rows, length), 0)
    return jnp.where(row_ids == index_row, 1.0, 0.0).astype(BF16)


def fill_lambda(hot, table_ref, wide_ref, diag_ref, factor):
    table = (table_ref[...] * factor).T
    hots = jnp.concatenate([hot, hot], axis=0)
    length = hot.shape[1]

    def wide_lams(level):
        columns = jnp.concatenate(
            [jnp.broadcast_to(table[:, n : n + 1], (table.shape[0], 128)) for n in (level, level + 1)], axis=1
        )
        value = mm(hots, jnp.concatenate(split3(columns)[:2], axis=0), TN)
        return value[:, :128], value[:, 128:]

    lams = [lam for level in range(0, 16, 2) for lam in wide_lams(level)]
    for level in range(wide_ref.shape[0]):
        wide_ref[level] = lams[9 + level]
    rows = lax.broadcasted_iota(jnp.int32, (128, 128), 0)
    cols = lax.broadcasted_iota(jnp.int32, (128, 128), 1)
    crossed = jnp.bitwise_xor(rows, cols)
    for level in range(8):
        lam = lams[level]
        for n in range(length // 128):
            tile, half = n // 2, n % 2
            spot = pl.ds(half * 128, 128)
            part = lam[n * 128 : (n + 1) * 128]
            if level == 0:
                diag_ref[tile, spot, spot] = jnp.where(cols <= rows, part, 0.0)
            else:
                low = 1 << (level - 1)
                diag_ref[tile, spot, spot] = jnp.where(
                    (crossed >= low) & (cols <= rows), part, diag_ref[tile, spot, spot]
                )
    lam = lams[8]
    for tile in range(length // SUB):
        diag_ref[tile, 0:128, 128:256] = jnp.zeros((128, 128), F32)
        diag_ref[tile, 128:256, 0:128] = lam[tile * SUB + 128 : (tile + 1) * SUB]


def row_sums(hot, value):
    high, rest, _ = split3(value)
    total = mm(hot, high, NN) + mm(hot, rest, NN)
    return jnp.sum(total, axis=1, keepdims=True)


def kernel(
    q_hbm, k_hbm, v_hbm, g_hbm, index_ref, table_ref,
    out_ref, qg_ref, kg_ref, vg_ref, total_ref,
    qb, kb, vb, gb, lout, lq, lk, lv, wide, diag, wsum, lsum, near, part, stack, pa, da, pb, db,
    states, sother, grads, gother, g0other, tree, recv, dsend, drecv, dtree, psum,
    in_sem, s_send, s_recv, g_send, g_recv, f_send, f_recv, r_send, r_recv,
    b_send, b_recv, d_send, d_recv, p_send, p_recv,
    *, factor, scale,
):
    heads, length, _ = qb.shape
    tiles = length // SUB
    half = heads // 2
    me = lax.axis_index("ctx")
    z = lax.axis_index("heads")
    core = me % 2
    y = (me // 2) % 4
    x = me // 8
    mine = core * half
    theirs = (1 - core) * half
    sibling = me + 1 - 2 * core
    at = lambda px, py: (px * 4 + py) * 2 + core
    hops = (at(x, y + 1 - 2 * (y % 2)), at(x, 3 - y), at(x + 1 - 2 * (x % 2), y), at(3 - x, y))
    bits = (core == 1, y % 2 == 1, y // 2 == 1, x % 2 == 1, x // 2 == 1)

    def pick(level):
        return jnp.where(level == 0, hops[0], jnp.where(level == 1, hops[1], jnp.where(level == 2, hops[2], hops[3])))

    def remote(src, dst, send, got, device):
        return pltpu.make_async_remote_copy(
            src_ref=src, dst_ref=dst, send_sem=send, recv_sem=got, device_id=device, device_id_type=MESH
        )

    loads = ((kb, k_hbm), (vb, v_hbm), (qb, q_hbm), (gb, g_hbm))

    def load(n, h):
        return pltpu.make_async_copy(loads[n][1].at[h], loads[n][0].at[h], in_sem.at[n, h])

    def load_pair(n, h):
        load(n, h).start()
        load(n + 1, h).start()

    for n in (0, 2):
        for u in range(half):
            load_pair(n, theirs + u)
            load_pair(n, mine + u)

    barrier = pltpu.get_barrier_semaphore()
    for d in range(1, 16):
        spot = (x * 4 + y + d) % 16
        pl.semaphore_signal(barrier, inc=1, device_id={"ctx": at(spot // 4, spot % 4)}, device_id_type=MESH)
    for d in range(1, 8):
        spot = (z * 2 + core + d) % 8
        device = {"ctx": me - core + spot % 2, "heads": spot // 2}
        pl.semaphore_signal(barrier, inc=1, device_id=device, device_id_type=MESH)

    def make_state(h):
        load(0, h).wait()
        load(1, h).wait()
        s = [mm(kb[h, pl.ds(c * SUB, SUB)], vb[h, pl.ds(c * SUB, SUB)], TN) for c in range(tiles)]
        pair = s[0] + s[1]
        near[h, 0] = s[0].astype(BF16)
        near[h, 1] = s[2].astype(BF16)
        near[h, 2] = pair.astype(BF16)
        states[h] = pair + (s[2] + s[3])

    def state_copy(u, low):
        block = states.at[low + u]
        return remote(block, sother.at[low + u], s_send.at[u], s_recv.at[u], {"ctx": sibling})

    def rest_copy(low):
        block = pl.ds(low, half)
        return remote(states.at[block], sother.at[block], s_send.at[half], s_recv.at[half], {"ctx": sibling})

    def make_grad(h, low, high):
        total = None
        for c in range(tiles):
            rows = pl.ds(c * SUB, SUB)
            wide_grad = gb[h, rows].astype(F32)
            scaled = jnp.concatenate([(wide[2 + j, rows] * wide_grad).astype(BF16) for j in range(low, high)], axis=1)
            value = mm(qb[h, rows], scaled, TN)
            total = value if total is None else total + value
        for j in range(low, high):
            grads[j, h] = jnp.where(bits[j], total[:, (j - low) * 128 : (j - low + 1) * 128], 0.0)

    def tree_copy(level, u):
        return remote(
            tree.at[level, u], recv.at[level, mine + u], f_send.at[level, u], f_recv.at[level, u], {"ctx": pick(level)}
        )

    def relay(level, u, low):
        block = recv.at[level, low + u]
        return remote(block, block, r_send.at[level, u], r_recv.at[level, u], {"ctx": sibling})

    def dtree_copy(level, u):
        return remote(
            dsend.at[level, u], drecv.at[level, u], b_send.at[level, u], b_recv.at[level, u], {"ctx": pick(level)}
        )

    def dtree_relay(u, low):
        block = dtree.at[low + u]
        return remote(block, block, d_send.at[u], d_recv.at[u], {"ctx": sibling})

    def grad_copy(u, low):
        return remote(
            grads.at[pl.ds(low, 2), theirs + u], gother.at[pl.ds(low - 1, 2), u],
            g_send.at[low // 2, u], g_recv.at[low // 2, u], {"ctx": sibling},
        )

    def grad0_copy():
        return remote(grads.at[0], g0other, g_send.at[2, 0], g_recv.at[2, 0], {"ctx": sibling})

    def start_tree(u):
        state_copy(u, mine).wait_recv()
        tree[0, u] = states[mine + u] + sother[mine + u]
        tree_copy(0, u).start()

    def start_dtree(u):
        grad_copy(u, 3).wait_recv()
        dsend[3, u] = grads[4, mine + u] + gother[3, u]
        dtree_copy(3, u).start()

    def tree_step(step):
        level = step // half
        u = step % half
        tree_copy(level, u).wait_recv()
        relay(level, u, mine).start()

        @pl.when(level < 3)
        def _():
            tree[level + 1, u] = tree[level, u] + recv[level, mine + u]
            tree_copy(level + 1, u).start()

    def dtree_step(step):
        level = step // half
        u = step % half
        back = 3 - level
        dtree_copy(back, u).wait_recv()

        @pl.when(level == 0)
        def _():
            dtree[mine + u] = drecv[back, u]

        @pl.when(level > 0)
        def _():
            dtree[mine + u] = dtree[mine + u] + drecv[back, u]

        @pl.when(level == 1)
        def _():
            grad_copy(u, 1).wait_recv()

        @pl.when(level < 3)
        def _():
            dsend[back - 1, u] = dtree[mine + u] + (grads[back, mine + u] + gother[back - 1, u])
            dtree_copy(back - 1, u).start()

        @pl.when(level == 3)
        def _():
            dtree_relay(u, mine).start()

    def state_step(u, carry):
        make_state(theirs + u)

        @pl.when(u == 0)
        def _():
            pl.semaphore_wait(barrier, PARTNERS)

        state_copy(u, theirs).start()
        make_state(mine + u)

        @pl.when(u >= 2)
        def _():
            start_tree(u - 2)

        return carry

    lax.fori_loop(0, half, state_step, 0)
    rest_copy(mine).start()
    start_tree(2)
    wsum[...] = jnp.zeros_like(wsum)
    lsum[...] = jnp.zeros_like(lsum)
    start_tree(3)
    hot = one_hot(index_ref[...], table_ref.shape[1])
    fill_lambda(hot, table_ref, wide, diag, factor)

    def grad_step(u, carry):
        load(2, theirs + u).wait()
        load(3, theirs + u).wait()
        make_grad(theirs + u, 0, 5)
        grad_copy(u, 3).start()
        grad_copy(u, 1).start()
        load(2, mine + u).wait()
        load(3, mine + u).wait()
        make_grad(mine + u, 0, 5)

        @pl.when(u >= 1)
        def _():
            start_dtree(u - 1)

        tree_step(u)
        return carry

    lax.fori_loop(0, half, grad_step, 0)
    grad0_copy().start()
    start_dtree(3)

    def tile_of(h, c):
        rows = pl.ds(c * SUB, SUB)
        return rows, qb[h, rows], kb[h, rows], vb[h, rows], gb[h, rows]

    def score_head(h, weighted, dscore):
        for c in range(tiles):
            rows, q, k, v, grad = tile_of(h, c)
            for part_rows, count in ((slice(0, 128), 128), (slice(128, 256), 256)):
                score = mm(q[part_rows], k[:count], NT)
                back = mm(grad[part_rows], v[:count], NT)
                spot = pl.ds(part_rows.start, 128)
                wsum[c, spot, 0:count] += score * back
                weight = diag[c, spot, 0:count]
                weighted[c, spot, 0:count] = (weight * score).astype(BF16)
                dscore[c, spot, 0:count] = (weight * back).astype(BF16)

    def local_head(h, weighted, dscore):
        near_grad = {}
        pair_grad = None
        for c in range(tiles - 1, -1, -1):
            rows, q, k, v, grad = tile_of(h, c)
            def lower(score, right):
                upper = mm(score[c, 0:128, 0:128], right[:128], NN)
                return jnp.concatenate([upper, mm(score[c, 128:256], right, NN)], axis=0)

            def lower_t(score, right):
                upper = mm(score[c, :, 0:128], right, TN)
                return jnp.concatenate([upper, mm(score[c, 128:256, 128:256], right[128:], TN)], axis=0)

            out = lower(weighted, v)
            qg = lower(dscore, k)
            kg = lower_t(dscore, q)
            vg = lower_t(weighted, grad)
            use = ([0] if c % 2 else []) + ([1] if c >= 2 else [])
            if use:
                buckets = ([near[h, c // 2]] if c % 2 else []) + ([near[h, 2]] if c >= 2 else [])
                joined = jnp.concatenate(buckets, axis=1)
                cross = mm(q, joined, NN)
                wide_grad = grad.astype(F32)
                scaled = []
                for n, level in enumerate(use):
                    piece = cross[:, n * 128 : (n + 1) * 128]
                    lam = wide[level, rows]
                    out += lam * piece
                    lsum[level, rows] += piece * wide_grad
                    scaled.append((lam * wide_grad).astype(BF16))
                scaled = jnp.concatenate(scaled, axis=1)
                qg += mm(scaled, joined, NT)
                value = mm(q, scaled, TN)
                for n, level in enumerate(use):
                    piece = value[:, n * 128 : (n + 1) * 128]
                    if level == 0:
                        near_grad[c - 1] = piece
                    else:
                        pair_grad = piece if pair_grad is None else pair_grad + piece
            dstate = near_grad.get(c)
            if c < 2:
                dstate = pair_grad if dstate is None else dstate + pair_grad
            if dstate is not None:
                part[h, c] = dstate
            lout[h, rows] = out
            lq[h, rows] = qg
            lk[h, rows] = kg
            lv[h, rows] = vg

    def comm_step(step):
        @pl.when((step >= TREE_LAG) & (step < TREE_LAG + 3 * half))
        def _():
            tree_step(step - TREE_LAG + half)

        @pl.when(step >= DTREE_LAG)
        def _():
            dtree_step(step - DTREE_LAG)

    def local_step(i, carry):
        h = 2 * i
        local_head(h, pa, da)
        score_head(h + 1, pb, db)
        comm_step(2 * h)
        comm_step(2 * h + 1)
        local_head(h + 1, pb, db)
        score_head(h + 2, pa, da)
        comm_step(2 * h + 2)
        comm_step(2 * h + 3)
        return carry

    score_head(0, pa, da)
    lax.fori_loop(0, heads // 2 - 1, local_step, 0)
    local_head(heads - 2, pa, da)
    score_head(heads - 1, pb, db)
    comm_step(2 * heads - 4)
    comm_step(2 * heads - 3)
    local_head(heads - 1, pb, db)
    comm_step(2 * heads - 2)
    comm_step(2 * heads - 1)

    lane = lax.broadcasted_iota(jnp.int32, (table_ref.shape[1], 128), 1)
    hot = one_hot(index_ref[...], table_ref.shape[1])
    rows_id = lax.broadcasted_iota(jnp.int32, (128, 128), 0)
    cols_id = lax.broadcasted_iota(jnp.int32, (128, 128), 1)
    crossed = jnp.bitwise_xor(rows_id, cols_id)
    table = jnp.zeros(lane.shape, F32)
    blocks = [wsum[n // 2, (n % 2) * 128 : (n % 2 + 1) * 128, (n % 2) * 128 : (n % 2 + 1) * 128] for n in range(2 * tiles)]
    high, rest, _ = split3(jnp.concatenate(blocks, axis=0))
    for level in range(8):
        low = (1 << (level - 1)) if level else 0
        mask = (crossed >= low) & (crossed < (1 << level)) & (cols_id <= rows_id)
        mask = jnp.where(mask, 1.0, 0.0).astype(BF16)
        mask = jnp.concatenate([mask] * (2 * tiles), axis=0)
        total = mm(hot, high * mask, NN) + mm(hot, rest * mask, NN)
        table = jnp.where(lane == level, jnp.sum(total, axis=1, keepdims=True), table)
    lower = [wsum[c, 128:256, 0:128] for c in range(tiles)]
    clear = jnp.zeros((128, 128), F32)
    lower = jnp.concatenate([piece for block in lower for piece in (clear, block)], axis=0)
    table = jnp.where(lane == 8, row_sums(hot, lower), table)
    for level in range(9, 11):
        table = jnp.where(lane == level, row_sums(hot, lsum[level - 9]), table)

    rest_copy(theirs).wait_recv()
    for level in range(4):
        for u in range(half):
            relay(level, u, theirs).wait_recv()

    def lam_step(h, carry):
        buckets = [jnp.where(bits[0], sother[h], 0.0).astype(BF16)]
        for j in range(1, 5):
            buckets.append(jnp.where(bits[j], recv[j - 1, h], 0.0).astype(BF16))
        stack[h] = jnp.concatenate(buckets, axis=0)
        joined = jnp.concatenate(buckets, axis=1)
        for c in range(tiles):
            rows = pl.ds(c * SUB, SUB)
            cross = mm(qb[h, rows], joined, NN)
            wide_grad = gb[h, rows].astype(F32)
            for j in range(5):
                lsum[2 + j, rows] += cross[:, j * 128 : (j + 1) * 128] * wide_grad
        return carry

    lax.fori_loop(0, heads, lam_step, 0)
    for level in range(11, 16):
        table = jnp.where(lane == level, row_sums(hot, lsum[level - 9]), table)

    spots = (z * 2 + core, x * 4 + y)
    sizes = (8, 16)
    psum[0, spots[0]] = (table * scale).T[0:16]

    def table_copy(phase, d):
        other = (spots[phase] + d) % sizes[phase]
        device = (
            {"ctx": me - core + other % 2, "heads": other // 2},
            {"ctx": at(other // 4, other % 4)},
        )[phase]
        slot = psum.at[phase, spots[phase]]
        return remote(slot, slot, p_send.at[phase, d - 1], p_recv.at[phase, d - 1], device)

    def table_wait(phase, d):
        other = (spots[phase] + sizes[phase] - d) % sizes[phase]
        slot = psum.at[phase, other]
        return remote(slot, slot, p_send.at[phase, d - 1], p_recv.at[phase, d - 1], {"ctx": sibling})

    for d in range(1, 8):
        table_copy(0, d).start()

    def table_phase(phase):
        for d in range(1, sizes[phase]):
            table_wait(phase, d).wait_recv()
        value = psum[phase, 0]
        for n in range(1, sizes[phase]):
            value = value + psum[phase, n]
        if phase < 1:
            psum[1, spots[1]] = value
            for d in range(1, 16):
                table_copy(1, d).start()
        else:
            total_ref[...] = value[:, 0:64]

    def out_step(h, carry):
        joined = jnp.concatenate([stack[h, j * 128 : (j + 1) * 128] for j in range(5)], axis=1)
        for c in range(tiles):
            rows = pl.ds(c * SUB, SUB)
            cross = mm(qb[h, rows], joined, NN)
            out = lout[h, rows]
            for j in range(5):
                out += wide[2 + j, rows] * cross[:, j * 128 : (j + 1) * 128]
            out_ref[h, rows] = out.astype(BF16)

        @pl.when(h < DTREE_LAG)
        def _():
            dtree_step(4 * half - DTREE_LAG + h)

        return carry

    lax.fori_loop(0, heads, out_step, 0)
    table_phase(0)
    for u in range(half):
        dtree_relay(u, theirs).wait_recv()
    grad0_copy().wait_recv()

    def grad_head(h):
        joined = stack[h]
        far = dtree[h] + jnp.where(bits[0], 0.0, g0other[h])
        for c in range(tiles):
            rows = pl.ds(c * SUB, SUB)
            back = mm(gb[h, rows], joined, NT)
            qg = lq[h, rows]
            for j in range(5):
                qg += wide[2 + j, rows] * back[:, j * 128 : (j + 1) * 128]
            dstate = (far + part[h, c] if c < 3 else far).astype(BF16)
            kg = lk[h, rows] + mm(vb[h, rows], dstate, NT)
            vg = lv[h, rows] + mm(kb[h, rows], dstate, NN)
            qg_ref[h, rows] = qg.astype(BF16)
            kg_ref[h, rows] = kg.astype(BF16)
            vg_ref[h, rows] = vg.astype(BF16)

    def grad_loop(low, high):
        def step(h, carry):
            grad_head(h)
            return carry

        lax.fori_loop(low, high, step, 0)

    grad_loop(0, heads)
    table_phase(1)

    rest_copy(mine).wait_send()
    grad0_copy().wait_send()
    for u in range(half):
        state_copy(u, theirs).wait_send()
        grad_copy(u, 1).wait_send()
        grad_copy(u, 3).wait_send()
        for level in range(4):
            tree_copy(level, u).wait_send()
            relay(level, u, mine).wait_send()
            dtree_copy(level, u).wait_send()
        dtree_relay(u, mine).wait_send()
    for phase in range(2):
        for d in range(1, sizes[phase]):
            table_copy(phase, d).wait_send()


def put_kernel(*refs):
    sems = refs[-1]
    count = (len(refs) - 1) // 2
    copies = []
    for n in range(count - 1):
        for h in range(0, refs[n].shape[0], 2):
            rows = pl.ds(h, 2)
            copies.append((refs[n].at[rows], refs[count + n].at[rows]))
    copies.append((refs[count - 1], refs[2 * count - 1]))
    copies = [pltpu.make_async_copy(src, dst, sems.at[i]) for i, (src, dst) in enumerate(copies)]
    for copy in copies:
        copy.start()
    for copy in copies:
        copy.wait()


def body(queries, keys, values, out_grad, level_table, table_index):
    heads, length, width = queries.shape
    devices = lax.axis_size("ctx")
    factor = 1.0 / math.sqrt(width * length * devices)
    tiles = length // SUB
    half = heads // 2
    dma = lambda *shape: pltpu.SemaphoreType.DMA(shape)
    square = (width, width)
    table_lanes = level_table.shape[0]
    outs = pl.pallas_call(
        functools.partial(kernel, factor=factor, scale=factor / math.sqrt(length * devices)),
        out_shape=tuple(pltpu.VMEM(queries.shape, BF16) for _ in range(4))
        + (pltpu.VMEM(level_table.shape[::-1], F32),),
        in_specs=[pl.BlockSpec(memory_space=pltpu.HBM)] * 4 + [pl.BlockSpec(memory_space=pltpu.VMEM)] * 2,
        out_specs=(pl.BlockSpec(memory_space=pltpu.VMEM),) * 5,
        scratch_shapes=[pltpu.VMEM(queries.shape, BF16)] * 4
        + [pltpu.VMEM(queries.shape, F32)] * 4
        + [
            pltpu.VMEM((7, length, 128), F32),
            pltpu.VMEM((tiles, SUB, SUB), F32),
            pltpu.VMEM((tiles, SUB, SUB), F32),
            pltpu.VMEM((7, length, 128), F32),
            pltpu.VMEM((heads, 3) + square, BF16),
            pltpu.VMEM((heads, 3) + square, F32),
            pltpu.VMEM((heads, 5 * width, width), BF16),
            pltpu.VMEM((tiles, SUB, SUB), BF16),
            pltpu.VMEM((tiles, SUB, SUB), BF16),
            pltpu.VMEM((tiles, SUB, SUB), BF16),
            pltpu.VMEM((tiles, SUB, SUB), BF16),
            pltpu.VMEM((heads,) + square, F32),
            pltpu.VMEM((heads,) + square, F32),
            pltpu.VMEM((5, heads) + square, F32),
            pltpu.VMEM((4, half) + square, F32),
            pltpu.VMEM((heads,) + square, F32),
            pltpu.VMEM((4, half) + square, F32),
            pltpu.VMEM((4, heads) + square, F32),
            pltpu.VMEM((4, half) + square, F32),
            pltpu.VMEM((4, half) + square, F32),
            pltpu.VMEM((heads,) + square, F32),
            pltpu.VMEM((2, 16, 16, table_lanes), F32),
            dma(4, heads), dma(half + 1), dma(half + 1), dma(3, half), dma(3, half),
            dma(4, half), dma(4, half), dma(4, half), dma(4, half),
            dma(4, half), dma(4, half), dma(half), dma(half), dma(2, 15), dma(2, 15),
        ],
        compiler_params=pltpu.CompilerParams(
            collective_id=0, has_side_effects=True, vmem_limit_bytes=54 << 20
        ),
    )(queries, keys, values, out_grad, table_index.reshape(1, length), level_table.T)
    outs = pl.pallas_call(
        put_kernel,
        out_shape=tuple(jax.ShapeDtypeStruct(queries.shape, BF16) for _ in range(4))
        + (jax.ShapeDtypeStruct(level_table.shape[::-1], F32),),
        in_specs=[pl.BlockSpec(memory_space=pltpu.VMEM)] * 5,
        out_specs=(pl.BlockSpec(memory_space=pltpu.HBM),) * 5,
        scratch_shapes=[dma(4 * heads // 2 + 1)],
        compiler_params=pltpu.CompilerParams(vmem_limit_bytes=1 << 20),
    )(*[pltpu.with_memory_space_constraint(value, pltpu.VMEM) for value in outs])
    return outs[:4] + (outs[4].T,)


def solution(mesh):
    placed = (P("heads", "ctx", None),) * 4
    return jax.shard_map(
        body,
        mesh=mesh,
        in_specs=placed + (P(), P("ctx")),
        out_specs=placed + (P(),),
        check_vma=False,
    )
```
